256 devices in a mesh: mom: 4 (over x_hi, core), en: 64 (over y, z, x_lo).
Axes of the slice: x: 4 (x_hi: 2, x_lo: 2; x = x_hi * 2 + x_lo), y: 4, z: 8, core: 2. Of those that a mesh axis runs over, the one named last changes fastest.
Arguments:
- green_less: bfloat16 [8, 1536, 8, 288], P('mom', 'en'), may hold values from -6 to 6
- green_greater: bfloat16 [8, 1536, 8, 288], P('mom', 'en'), may hold values from -6 to 6
- derivative: float32 [2, 3, 144], replicated, may hold values from -1.75 to 1.75
- neighbours: int32 [2, 4], replicated, may hold values from 0 to 1
- phonon: bfloat16 [2, 8, 24, 3, 8], replicated, may hold values from 0.0099487305 to 0.099609375
Outputs:
- self_energy: bfloat16 [8, 1536, 8, 288], P('mom', 'en')
- polarisation: float32 [8, 24, 3, 8], P('mom')
The draws below stay inside these ranges and needn't reach their ends.
All inputs are finite; a program needn't handle non-finite values.
Results may differ from the reference program's by a relative error of at most 0.0034.
Values may be sent and summed in bfloat16 or wider, within the bound.
A program may use at most 64 MiB of HBM per device.

```python
import math
import jax
import jax.numpy as jnp
from jax import lax

NO = 12
NB = 4
A = 2
W = 24
ED = 24
K = 8
NE = 1536
P_SIZE = 8


def draw_green_less(key, part):
    energy = jnp.arange(NE, dtype=jnp.float32) / NE
    shape = (K, NE, A * NB, 2 * NO * NO)
    scale = 0.5 + energy
    values = jax.random.normal(key, shape, jnp.float32) * scale[None, :, None, None]
    return jnp.clip(values, -6.0, 6.0).astype(jnp.bfloat16)


def touch_ends(drawn, stream_key, smallest, largest):
    extent = drawn.shape
    place = [jax.random.randint(jax.random.fold_in(stream_key, axis), (), 0, extent[axis]) for axis in range(len(extent))]
    drawn = drawn.at[tuple(place)].set(smallest)
    longest = extent.index(max(extent))
    place[longest] = (place[longest] + 1) % extent[longest]
    return drawn.at[tuple(place)].set(largest)


def levels(rng, shape, pieces, smallest, largest):
    loudness, own = 1.0, jax.random.fold_in(rng, 6)
    for axis_at, parts in pieces:
        draws = jnp.exp(jax.random.uniform(jax.random.fold_in(own, axis_at), (parts,), jnp.float32, smallest / len(pieces), largest / len(pieces)))
        loudness = loudness * jnp.repeat(draws, shape[axis_at] // parts).reshape([-1 if axis == axis_at else 1 for axis in range(len(shape))])
    return loudness


def bell_draw(rng, dims, spread, reach, cuts=(), kind=jnp.bfloat16):
    factor_of = levels(rng, dims, cuts, -0.22, 0.18) if cuts else 1.0
    values = jax.random.normal(rng, dims, jnp.float32) * spread * factor_of
    return jnp.minimum(jnp.maximum(values, -reach), reach).astype(kind)


def setup_inputs(seed: int = 0) -> dict:
    seeds = jax.random.split(jax.random.key(seed), 6)
    return {
        "green_less": draw_green_less(jax.random.fold_in(seeds[5], 71), 0),
        "green_greater": bell_draw(seeds[1], (K, NE, P_SIZE, 2 * NO * NO), 1.0, 6.0, ((0, 4), (1, 64))),
        "derivative": bell_draw(seeds[2], (A, 3, NO * NO), NO ** -0.5, 1.75, (), jnp.float32),
        "neighbours": touch_ends(jax.random.randint(seeds[3], (A, NB), 0, A), jax.random.fold_in(seeds[3], 1), 0, A - 1).astype(jnp.int32),
        "phonon": jnp.clip(jnp.exp(jax.random.uniform(seeds[4], (2, K, W, 3, P_SIZE), jnp.float32, math.log(0.0099487305), math.log(0.099609375))), 0.0099487305, 0.099609375).astype(jnp.bfloat16),
    }


HIGHEST = lax.Precision.HIGHEST

def band_table(length_out, length_in, depth_count):
    row_index = jnp.arange(length_out, dtype=jnp.int32)[:, None, None]
    col_index = jnp.arange(length_in, dtype=jnp.int32)[None, :, None]
    offsets = jnp.arange(depth_count, dtype=jnp.int32)[None, None, :]
    return (col_index - row_index == offsets).astype(jnp.float32)

def reference(green_less, green_greater, derivative, neighbours, phonon):
    pair_count = A * NB
    matrices = derivative.reshape(A, 3, NO, NO)
    left_blocks = jnp.repeat(matrices, NB, axis=0)
    right_blocks = matrices[neighbours.reshape(-1).astype(jnp.int32)]
    kernel = jnp.concatenate([jnp.flip(phonon[0], 1), jnp.zeros((K, 1, 3, pair_count), phonon.dtype), phonon[1]], axis=1).astype(jnp.float32)
    toeplitz = jnp.einsum('kimp,eji->kpmej', kernel, band_table(ED, ED + 2 * W, 2 * W + 1))
    selector = band_table(ED, ED + W - 1, W)
    padded = jnp.pad(green_less, ((0, 0), (W, W), (0, 0), (0, 0)))
    sign_pair = jnp.array([1.0, -1.0], jnp.float32)

    def one_block(block_index):
        first_row = (block_index * ED).astype(jnp.int32)
        window = lax.dynamic_slice_in_dim(padded, first_row, ED + 2 * W, 1).astype(jnp.float32)
        greater = lax.dynamic_slice_in_dim(green_greater, first_row, ED, 1).astype(jnp.float32)
        greater = greater.reshape(K, ED, pair_count, 2, NO, NO)
        half_product = jnp.einsum('kepcui,pmis->kepmcus', greater, left_blocks, precision=HIGHEST)
        weighted = jnp.einsum('kepmcus,pmut->kepmcst', half_product, right_blocks, precision=HIGHEST)
        weighted = weighted * sign_pair[:, None, None]
        weighted = lax.optimization_barrier(weighted.astype(jnp.bfloat16)).astype(jnp.float32)
        weighted = weighted.reshape(K, ED, pair_count, 3, 2 * NO * NO)
        upper_rows = window[:, W + 1:]
        window_sum = jnp.zeros((K, ED, pair_count, 3, 2 * NO * NO), jnp.float32)
        polar_rows = []
        for momentum in range(K):
            window_sum = window_sum + jnp.einsum('pmej,kjpx->kepmx', toeplitz[momentum], jnp.roll(window, momentum, axis=0))
            pair_sums = jnp.einsum('kjpx,kepmx->pmje', jnp.roll(upper_rows, -momentum, axis=0), weighted)
            polar_rows.append(jnp.einsum('pmje,ejw->wmp', pair_sums, selector, precision=HIGHEST))
        product_left = jnp.einsum('pmis,kepmcst->kepmcit', left_blocks, window_sum.reshape(K, ED, pair_count, 3, 2, NO, NO), precision=HIGHEST)
        energy = jnp.einsum('kepmcit,pmut->kepciu', product_left, right_blocks, precision=HIGHEST)
        energy = energy.reshape(K, ED, pair_count, 2 * NO * NO).astype(jnp.bfloat16)
        return (energy, jnp.stack(polar_rows))
    block_energy, block_polar = lax.map(one_block, jnp.arange(NE // ED, dtype=jnp.int32))
    self_energy = jnp.moveaxis(block_energy, 0, 1).reshape(K, NE, pair_count, 2 * NO * NO)
    polarisation = lax.optimization_barrier(jnp.sum(block_polar, axis=0)) / (NO * jnp.sqrt(jnp.float32(K * NE)))
    return (self_energy, polarisation)
```

```python
import functools

import jax
import jax.numpy as jnp
import numpy as np
from jax import lax
from jax.experimental import pallas as pl
from jax.experimental.pallas import tpu as pltpu
from jax.sharding import PartitionSpec as P

NO = 12
NB = 4
NN = NO * NO
MESH = pl.DeviceIdType.MESH
BF = jnp.bfloat16
F32 = jnp.float32


def tables(momenta, window):
    r = np.arange(NN)
    col = np.arange(2 * NN)
    sub = col % NN
    rows_s = (r[None, :] % NO == r[:, None] // NO).astype(np.float32)
    rows_t = (r[None, :] % NO == r[:, None] % NO).astype(np.float32)
    cols_i = (r[:, None] // NO == sub[None, :] // NO).astype(np.float32)
    cols_u = (r[:, None] // NO == sub[None, :] % NO).astype(np.float32)
    flipped = (col // NN) * NN + (sub % NO) * NO + sub // NO
    swap = np.zeros((2 * NN, 2 * NN), np.float32)
    swap[flipped, col] = np.where(col < NN, 1.0, -1.0)
    place = np.zeros((2, momenta, window, 5, 32 * momenta), np.float32)
    for block in range(momenta):
        q = (-block) % momenta
        for de in range(window):
            at = 32 * block + de
            place[0, q, window - 1 - de, 0, at] = 1.0
            if de >= 1:
                place[1, q, de - 1, 1, at] = 1.0
            if de == 0:
                place[1, q, window - 1, 3, at] = 1.0
        for de in range(1 - window, 0):
            at = (32 * block + de) % (32 * momenta)
            place[0, q, -de - 1, 2, at] = 1.0
            place[1, q, window - 1 + de, 4, at] = 1.0
    place = place.reshape(2 * momenta * window, 5 * 32 * momenta)
    return rows_s, rows_t, cols_i, cols_u, swap, place


def kernel(
    dims,
    gl_ref, gg_ref, der_ref, nb_ref, coef_ref, rs_ref, rt_ref, ci_ref, cu_ref, swap_ref,
    se_ref, pol_ref,
    rows_f, gl_t, gg_t, gl, gg, toe, kr_hi, kr_lo, wgt, acc, se_t, se_r, part, got_z, plane, got_p,
    s_gg, r_gg, s_gl, r_gl, s_se, r_se, s_z, r_z, s_p, r_p,
):
    moms, ens, ny, nz, nx, own_k, own_e, pairs, momenta = dims
    pp_n = pairs // moms
    rows = own_k * own_e
    all_rows = momenta * own_e
    me = lax.axis_index("mom")
    en = lax.axis_index("en")
    iy, iz, ix = en // (nz * nx), (en // nx) % nz, en % nx
    up, down = lax.rem(en + 1, ens), lax.rem(en + ens - 1, ens)

    gl[:, :, :, own_e:, :] = jnp.zeros((3, pp_n, momenta, 32 - own_e, 2 * NN), BF)

    barrier = pltpu.get_barrier_semaphore()

    def greet(mom_at, en_at):
        pl.semaphore_signal(
            barrier, inc=1, device_id={"mom": mom_at, "en": en_at}, device_id_type=MESH
        )

    for rel in range(1, moms):
        greet(lax.rem(me + rel, moms), en)
    for rel in range(moms):
        greet(lax.rem(me + rel, moms), up)
        greet(lax.rem(me + rel, moms), down)
    for rel in range(1, nz):
        greet(me, (iy * nz + lax.rem(iz + rel, nz)) * nx + ix)
    plane_n = ny * nx * moms

    def plane_peer(rel):
        ry, rx, rm = rel // (nx * moms), (rel // moms) % nx, rel % moms
        oy, ox, om = lax.rem(iy + ry, ny), lax.rem(ix + rx, nx), lax.rem(me + rm, moms)
        return om, (oy * nz + iz) * nx + ox, (oy * nx + ox) * moms + om

    @pl.loop(1, plane_n)
    def _(rel):
        om, oe, _ = plane_peer(rel)
        greet(om, oe)

    chunks = [(at, min(128, 2 * NN - at)) for at in range(0, 2 * NN, 128)]

    for src, dst in ((gg_ref, gg_t), (gl_ref, gl_t)):
        whole = src[...].astype(F32).reshape(rows * pairs, 2 * NN)
        for c, (at, wide) in enumerate(chunks):
            rows_f[c, :, :wide] = whole[:, at : at + wide]
        for p in range(pairs):
            block = jnp.concatenate(
                [
                    rows_f.at[c][pl.ds(p, rows, stride=pairs), :][:, :wide]
                    for c, (_, wide) in enumerate(chunks)
                ],
                axis=1,
            ).astype(BF)
            dst[p] = block.reshape(dst.shape[1:])
    for pp in range(pp_n):
        gg[pp, pl.ds(pl.multiple_of(me * rows, 16), rows), :] = gg_t[me * pp_n + pp]
        gl[1, pp, pl.ds(me * own_k, own_k), pl.ds(0, own_e), :] = gl_t[me * pp_n + pp]

    pl.semaphore_wait(barrier, 3 * moms - 1 + nz - 1 + plane_n - 1)

    def gg_copy(rel):
        to = lax.rem(me + rel, moms)
        return pltpu.make_async_remote_copy(
            src_ref=gg_t.at[pl.ds(to * pp_n, pp_n)],
            dst_ref=gg.at[:, pl.ds(pl.multiple_of(me * rows, 16), rows), :],
            send_sem=s_gg.at[rel], recv_sem=r_gg.at[me],
            device_id={"mom": to, "en": en}, device_id_type=MESH,
        )

    def gl_copy(slot, rel, target):
        to = lax.rem(me + rel, moms)
        return pltpu.make_async_remote_copy(
            src_ref=gl_t.at[pl.ds(to * pp_n, pp_n)],
            dst_ref=gl.at[slot, :, pl.ds(me * own_k, own_k), pl.ds(0, own_e), :],
            send_sem=s_gl.at[slot, rel], recv_sem=r_gl.at[slot, me],
            device_id={"mom": to, "en": target}, device_id_type=MESH,
        )

    sent = [gg_copy(rel) for rel in range(1, moms)]
    sent += [gl_copy(1, rel, en) for rel in range(1, moms)]
    sent += [gl_copy(2, rel, down) for rel in range(moms)]
    sent += [gl_copy(0, rel, up) for rel in range(moms)]
    for copy in sent:
        copy.start()

    def await_gg():
        for rel in range(1, moms):
            at = lax.rem(me + rel, moms)
            view = gg.at[:, pl.ds(pl.multiple_of(at * rows, 16), rows), :]
            pltpu.make_async_copy(view, view, r_gg.at[at]).wait()

    def await_gl(slot):
        for rel in range(1 if slot == 1 else 0, moms):
            at = lax.rem(me + rel, moms)
            view = gl.at[slot, :, pl.ds(at * own_k, own_k), pl.ds(0, own_e), :]
            pltpu.make_async_copy(view, view, r_gl.at[slot, at]).wait()

    first_part = lax.broadcasted_iota(jnp.int32, (NN, 2 * NN), 1) < NN

    def split(x):
        hi = x.astype(BF)
        return hi, (x - hi.astype(F32)).astype(BF)

    def expand(row, rows_of, cols_of):
        hi, lo = split(row)
        out = jnp.dot(rows_of * hi, cols_of, preferred_element_type=F32)
        return out + jnp.dot(rows_of * lo, cols_of, preferred_element_type=F32)

    atom = (me * pp_n) // NB
    lefts = [
        expand(der_ref[atom, pl.ds(m, 1), :], rs_ref[...], ci_ref[...]) for m in range(3)
    ]
    for pp in range(pp_n):
        pair = me * pp_n + pp
        other = nb_ref[pair // NB, lax.rem(pair, NB)]
        for m in range(3):
            right = expand(der_ref[other, pl.ds(m, 1), :], rt_ref[...], cu_ref[...])
            both = lefts[m] * right
            for half, keep in ((0, first_part), (1, jnp.logical_not(first_part))):
                hi, lo = split(jnp.where(keep, both, 0.0))
                kr_hi[pp, m, NN * half : NN * (half + 1), :] = hi
                kr_lo[pp, m, NN * half : NN * (half + 1), :] = lo

    lane = lax.broadcasted_iota(jnp.int32, (own_e, 128), 1)
    row = lax.broadcasted_iota(jnp.int32, (own_e, 128), 0)
    spot = lax.rem(lane, 32)

    def turn(lo, hi, blocks):
        blocks = blocks % 8
        if blocks >= 4:
            lo, hi, blocks = hi, lo, blocks - 4
        if blocks == 0:
            return lo, hi
        a, b = pltpu.roll(lo, 32 * blocks, 1), pltpu.roll(hi, 32 * blocks, 1)
        keep = lane >= 32 * blocks
        return jnp.where(keep, a, b), jnp.where(keep, b, a)

    def slide(vector):
        lo = jnp.broadcast_to(vector[:, :128], (own_e, 128))
        hi = jnp.broadcast_to(vector[:, 128:], (own_e, 128))
        a = pltpu.roll(lo, 0, 1, stride=1, stride_axis=0)
        b = pltpu.roll(hi, 0, 1, stride=1, stride_axis=0)
        keep = lane >= row
        return jnp.where(keep, a, b), jnp.where(keep, b, a)

    span = 32 * momenta
    has_low = (en > 0).astype(F32)
    has_up = (en < ens - 1).astype(F32)
    zeros = jnp.zeros((1, span), F32)
    for pp in range(pp_n):
        for m in range(3):
            vec = coef_ref[me * pp_n + pp, pl.ds(m, 1), :]
            part_of = [vec[:, span * i : span * (i + 1)] for i in range(5)]
            combos = (
                (part_of[0] * has_low, zeros),
                (part_of[1], part_of[2]),
                (part_of[3] * has_up, part_of[4] * has_up),
            )
            for slot, (plus, minus) in enumerate(combos):
                plus, minus = slide(plus), slide(minus)
                lo = jnp.where(spot >= row, plus[0], minus[0])
                hi = jnp.where(spot >= row, plus[1], minus[1])
                for k in range(0, momenta, 2):
                    even, odd = turn(lo, hi, k), turn(lo, hi, k + 1)
                    at = m * all_rows + k * own_e
                    for side in range(2):
                        both = jnp.concatenate([even[side], odd[side]], axis=0)
                        toe[slot, pp, at : at + 2 * own_e, 128 * side : 128 * (side + 1)] = (
                            both.astype(BF)
                        )

    nt = (((1,), (1,)), ((), ()))
    await_gg()
    for pp in range(pp_n):
        swapped = jnp.dot(gg[pp], swap_ref[...], preferred_element_type=F32).astype(BF)
        for m in range(3):
            w = lax.dot_general(swapped, kr_hi[pp, m], nt, preferred_element_type=F32)
            w = w + lax.dot_general(swapped, kr_lo[pp, m], nt, preferred_element_type=F32)
            wgt[pp, m] = w.astype(BF)

    def window(slot, pp):
        g = gl[slot, pp].reshape(span, 2 * NN)
        for m in range(3):
            t = toe[slot, pp, m * all_rows : (m + 1) * all_rows, :]
            h = jnp.dot(t, g, preferred_element_type=F32)
            if slot == 1:
                acc[pp, m] = h
            else:
                acc[pp, m] += h

    def pair_sums(slot, pp, m):
        g = gl[slot, pp].reshape(span, 2 * NN)
        z = lax.dot_general(wgt[pp, m], g, nt, preferred_element_type=F32)
        total = None
        for k in range(4):
            a = z[own_e * k : own_e * (k + 1)]
            b = z[own_e * (k + 4) : own_e * (k + 5)]
            lo, hi = turn(a[:, :128] + b[:, 128:], a[:, 128:] + b[:, :128], 8 - k)
            total = (lo, hi) if total is None else (total[0] + lo, total[1] + hi)
        return total

    step = lax.broadcasted_iota(jnp.int32, (8, 128), 0)

    def diagonals(a, b):
        total = None
        for at in range(0, own_e, 8):
            x = pltpu.roll(a[at : at + 8], (127 - at) % 128, 1)
            x = x + pltpu.roll(b[at : at + 8], (127 + own_e - at) % 128, 1)
            total = x if total is None else total + x
        for bit in (1, 2, 4):
            total = jnp.where(step & bit != 0, pltpu.roll(total, 128 - bit, 1), total)
        return total

    await_gl(1)
    own_sums = {(pp, m): pair_sums(1, pp, m) for pp in range(pp_n) for m in range(3)}
    await_gl(2)
    lines = []
    scale = 1.0 / (NO * np.sqrt(np.float32(momenta * ens * own_e)))
    for pp in range(pp_n):
        for m in range(3):
            above = pair_sums(2, pp, m)
            line = []
            for side in range(2):
                a = jnp.where(spot > row, own_sums[pp, m][side], 0.0)
                b = jnp.where(spot <= row, above[side] * has_up, 0.0)
                line.append(jnp.sum(diagonals(a, b), axis=0, keepdims=True) * scale)
            lines.append(jnp.concatenate(line, axis=1))
    lines.append(jnp.zeros((8 - len(lines), span), F32))
    part[...] = jnp.concatenate(lines, axis=0)
    got_z[iz] = part[...]

    def z_copy(rel):
        to = lax.rem(iz + rel, nz)
        return pltpu.make_async_remote_copy(
            src_ref=part, dst_ref=got_z.at[iz],
            send_sem=s_z.at[rel], recv_sem=r_z.at[iz],
            device_id={"mom": me, "en": (iy * nz + to) * nx + ix}, device_id_type=MESH,
        )

    z_sent = [z_copy(rel) for rel in range(1, nz)]
    for copy in z_sent:
        copy.start()

    for pp in range(pp_n):
        window(1, pp)
        window(2, pp)
    await_gl(0)
    for pp in range(pp_n):
        window(0, pp)
        se = None
        for m in range(3):
            hi, lo = split(acc[pp, m])
            for x, y in ((hi, kr_hi), (lo, kr_hi), (hi, kr_lo)):
                term = jnp.dot(x, y[pp, m], preferred_element_type=F32)
                se = term if se is None else se + term
        se_t[pp] = se.astype(BF)
        se_r[me * pp_n + pp] = se_t[pp, pl.ds(pl.multiple_of(me * rows, 16), rows), :]

    def se_copy(rel):
        to = lax.rem(me + rel, moms)
        return pltpu.make_async_remote_copy(
            src_ref=se_t.at[:, pl.ds(pl.multiple_of(to * rows, 16), rows), :],
            dst_ref=se_r.at[pl.ds(me * pp_n, pp_n)],
            send_sem=s_se.at[rel], recv_sem=r_se.at[me],
            device_id={"mom": to, "en": en}, device_id_type=MESH,
        )

    se_sent = [se_copy(rel) for rel in range(1, moms)]
    for copy in se_sent:
        copy.start()

    for rel in range(1, nz):
        at = lax.rem(iz + rel, nz)
        pltpu.make_async_copy(part, got_z.at[at], r_z.at[at]).wait()
    total = got_z[0]
    for z in range(1, nz):
        total = total + got_z[z]
    plane[0] = total[:, :128]
    plane[1] = total[:, 128:]
    mine = (iy * nx + ix) * moms + me
    got_p[mine] = plane[me // 2]

    def p_copy(rel):
        om, oe, _ = plane_peer(rel)
        return pltpu.make_async_remote_copy(
            src_ref=plane.at[om // 2], dst_ref=got_p.at[mine],
            send_sem=s_p.at[rel], recv_sem=r_p.at[mine],
            device_id={"mom": om, "en": oe}, device_id_type=MESH,
        )

    @pl.loop(1, plane_n)
    def _(rel):
        p_copy(rel).start()

    for rel in range(1, moms):
        at = lax.rem(me + rel, moms)
        view = se_r.at[pl.ds(at * pp_n, pp_n)]
        pltpu.make_async_copy(view, view, r_se.at[at]).wait()
    for p in range(pairs):
        block = se_r[p].astype(F32)
        block = jnp.concatenate([block, jnp.zeros((rows, 384 - 2 * NN), F32)], axis=1)
        for c, (at, _) in enumerate(chunks):
            rows_f.at[c][pl.ds(p, rows, stride=pairs), :] = block[:, at : at + 128]
    whole = jnp.concatenate([rows_f[c, :, :wide] for c, (_, wide) in enumerate(chunks)], axis=1)
    se_ref[...] = whole.reshape(own_k, own_e, pairs, 2 * NN).astype(BF)

    @pl.loop(1, plane_n)
    def _(rel):
        _, _, slot = plane_peer(rel)
        pltpu.make_async_copy(got_p.at[slot], got_p.at[slot], r_p.at[slot]).wait()

    odd = lax.rem(me, 2) == 1
    for a in range(moms):
        total = got_p[a]
        for i in range(1, ny * nx):
            total = total + got_p[i * moms + a]
        pol_ref[a] = jnp.where(odd, pltpu.roll(total, 64, 1), total)

    for copy in sent + z_sent + se_sent:
        copy.wait_send()

    @pl.loop(1, plane_n)
    def _(rel):
        p_copy(rel).wait_send()


def body(green_less, green_greater, derivative, neighbours, phonon):
    own_k, own_e, pairs, width = green_less.shape
    momenta, window = phonon.shape[1], phonon.shape[2]
    moms, ens = lax.axis_size("mom"), lax.axis_size("en")
    nx = 2
    nz = min(8, ens // nx)
    ny = ens // (nz * nx)
    dims = (moms, ens, ny, nz, nx, own_k, own_e, pairs, momenta)
    pp_n = pairs // moms
    span = 32 * momenta
    rs, rt, ci, cu, swap, place = (jnp.asarray(t, BF) for t in tables(momenta, window))
    coef = jnp.einsum(
        "rmp,rl->pml", phonon.reshape(2 * momenta * window, 3, pairs), place,
        preferred_element_type=F32,
    )
    vm = pl.BlockSpec(memory_space=pltpu.VMEM)
    rows = own_k * own_e
    all_rows = momenta * own_e
    dma = pltpu.SemaphoreType.DMA
    plane_n = ny * nx * moms
    self_energy, pol = pl.pallas_call(
        functools.partial(kernel, dims),
        out_shape=(
            jax.ShapeDtypeStruct((own_k, own_e, pairs, width), BF),
            jax.ShapeDtypeStruct((moms, 8, 128), F32),
        ),
        in_specs=[vm, vm, vm, pl.BlockSpec(memory_space=pltpu.SMEM)] + [vm] * 6,
        out_specs=(vm, vm),
        scratch_shapes=[
            pltpu.VMEM((3, rows * pairs, 128), F32),
            pltpu.VMEM((pairs, own_k, own_e, width), BF),
            pltpu.VMEM((pairs, rows, width), BF),
            pltpu.VMEM((3, pp_n, momenta, 32, width), BF),
            pltpu.VMEM((pp_n, all_rows, width), BF),
            pltpu.VMEM((3, pp_n, 3 * all_rows, span), BF),
            pltpu.VMEM((pp_n, 3, width, width), BF),
            pltpu.VMEM((pp_n, 3, width, width), BF),
            pltpu.VMEM((pp_n, 3, all_rows, width), BF),
            pltpu.VMEM((pp_n, 3, all_rows, width), F32),
            pltpu.VMEM((pp_n, all_rows, width), BF),
            pltpu.VMEM((pairs, rows, width), BF),
            pltpu.VMEM((8, span), F32),
            pltpu.VMEM((nz, 8, span), F32),
            pltpu.VMEM((2, 8, 128), F32),
            pltpu.VMEM((plane_n, 8, 128), F32),
            dma((moms,)), dma((moms,)), dma((3, moms)), dma((3, moms)),
            dma((moms,)), dma((moms,)), dma((nz,)), dma((nz,)), dma((plane_n,)), dma((plane_n,)),
        ],
        compiler_params=pltpu.CompilerParams(collective_id=0, has_side_effects=True),
    )(green_less, green_greater, derivative, neighbours, coef, rs, rt, ci, cu, swap)
    pol = pol[:, : 3 * pp_n, :64].reshape(moms, pp_n, 3, momenta // moms, 32)[..., :window]
    pol = pol.transpose(3, 4, 2, 0, 1).reshape(momenta // moms, window, 3, pairs)
    return self_energy, pol


def solution(mesh):
    return jax.shard_map(
        body,
        mesh=mesh,
        in_specs=(P("mom", "en", None, None), P("mom", "en", None, None), P(), P(), P()),
        out_specs=(P("mom", "en", None, None), P("mom", None, None, None)),
        check_vma=False,
    )
```

```python
import functools

import jax
import jax.numpy as jnp
import numpy as np
from jax import lax
from jax.experimental import pallas as pl
from jax.experimental.pallas import tpu as pltpu
from jax.sharding import PartitionSpec as P

NO = 12
NB = 4
NN = NO * NO
MAIN = 256
TAIL = 2 * NN - MAIN
WIDE = MAIN + 128
MESH = pl.DeviceIdType.MESH
BF = jnp.bfloat16
F32 = jnp.float32
NT = (((1,), (1,)), ((), ()))


def tables(pp_n):
    r = np.arange(NN)
    col = np.arange(2 * NN)
    sub = col % NN
    rows_s = (r[None, :] % NO == r[:, None] // NO).astype(np.float32)
    rows_t = (r[None, :] % NO == r[:, None] % NO).astype(np.float32)
    cols_i = np.zeros((NN, WIDE), np.float32)
    cols_u = np.zeros((NN, WIDE), np.float32)
    cols_i[:, : 2 * NN] = r[:, None] // NO == sub[None, :] // NO
    cols_u[:, : 2 * NN] = r[:, None] // NO == sub[None, :] % NO
    swap = np.zeros((pp_n, WIDE, WIDE), np.float32)
    flipped = (col // NN) * NN + (sub % NO) * NO + sub // NO
    for pp in range(pp_n):
        at = np.where(col < MAIN, col, col + TAIL * pp)
        swap[pp, at[flipped], at] = np.where(col < NN, 1.0, -1.0)
    return rows_s, rows_t, cols_i, cols_u, swap


def split(x):
    hi = x.astype(BF)
    return hi, (x - hi.astype(F32)).astype(BF)


def kernel(
    dims,
    gl_ref, gg_ref, der_ref, nb_ref, ph_ref, rs_ref, rt_ref, ci_ref, cu_ref, swap_ref,
    se_r, pol_ref,
    rows_f, gl_t, gg_t, gl, gg, coef, toe, kr_hi, kr_lo, wgt, acc, se_t, part, got_z, plane, got_p,
    s_gg, r_gg, s_gl, r_gl, s_se, r_se, s_z, r_z, s_p, r_p,
):
    moms, ens, ny, nz, nx, own_k, own_e, pairs, momenta, window_n = dims
    pp_n = pairs // moms
    rows = own_k * own_e
    all_rows = momenta * own_e
    span = 32 * momenta
    cols = MAIN * pp_n + 128
    me = lax.axis_index("mom")
    en = lax.axis_index("en")
    iy, iz, ix = en // (nz * nx), (en // nx) % nz, en % nx
    up, down = lax.rem(en + 1, ens), lax.rem(en + ens - 1, ens)

    gl[:, :, own_e:, :] = jnp.zeros((3, momenta, 32 - own_e, cols), BF)

    barrier = pltpu.get_barrier_semaphore()

    def greet(mom_at, en_at):
        pl.semaphore_signal(
            barrier, inc=1, device_id={"mom": mom_at, "en": en_at}, device_id_type=MESH
        )

    for rel in range(1, moms):
        greet(lax.rem(me + rel, moms), en)
    for rel in range(moms):
        greet(lax.rem(me + rel, moms), up)
        greet(lax.rem(me + rel, moms), down)
    for rel in range(1, nz):
        greet(me, (iy * nz + lax.rem(iz + rel, nz)) * nx + ix)
    plane_n = ny * nx * moms

    def plane_peer(rel):
        ry, rx, rm = rel // (nx * moms), (rel // moms) % nx, rel % moms
        oy, ox, om = lax.rem(iy + ry, ny), lax.rem(ix + rx, nx), lax.rem(me + rm, moms)
        return om, (oy * nz + iz) * nx + ox, (oy * nx + ox) * moms + om

    @pl.loop(1, plane_n)
    def _(rel):
        om, oe, _ = plane_peer(rel)
        greet(om, oe)

    tail_lane = lax.broadcasted_iota(jnp.int32, (rows, 128), 1)

    def by_pair(src, dst):
        whole = src[...].astype(F32).reshape(rows * pairs, 2 * NN)
        rows_f[0] = whole[:, :128]
        rows_f[1] = whole[:, 128:MAIN]
        rows_f[2, :, :TAIL] = whole[:, MAIN:]
        for a in range(moms):
            tail = jnp.zeros((rows, 128), F32)
            parts = []
            for pp in range(pp_n):
                x = [rows_f.at[c][pl.ds(a * pp_n + pp, rows, stride=pairs), :] for c in range(3)]
                parts += x[:2]
                last = pltpu.roll(x[2], TAIL * pp, 1) if pp else x[2]
                keep = (tail_lane >= TAIL * pp) & (tail_lane < TAIL * (pp + 1))
                tail = jnp.where(keep, last, tail)
            block = jnp.concatenate(parts + [tail], axis=1).astype(BF)
            dst[a] = block.reshape(dst.shape[1:])

    by_pair(gg_ref, gg_t)
    pl.semaphore_wait(barrier, 3 * moms - 1 + nz - 1 + plane_n - 1)

    def gg_copy(rel):
        to = lax.rem(me + rel, moms)
        return pltpu.make_async_remote_copy(
            src_ref=gg_t.at[to],
            dst_ref=gg.at[pl.ds(pl.multiple_of(me * rows, 16), rows), :],
            send_sem=s_gg.at[rel], recv_sem=r_gg.at[me],
            device_id={"mom": to, "en": en}, device_id_type=MESH,
        )

    def gl_copy(slot, rel, target):
        to = lax.rem(me + rel, moms)
        return pltpu.make_async_remote_copy(
            src_ref=gl_t.at[to],
            dst_ref=gl.at[slot, pl.ds(me * own_k, own_k), pl.ds(0, own_e), :],
            send_sem=s_gl.at[slot, rel], recv_sem=r_gl.at[slot, me],
            device_id={"mom": to, "en": target}, device_id_type=MESH,
        )

    sent = [gg_copy(rel) for rel in range(1, moms)]
    for copy in sent:
        copy.start()
    by_pair(gl_ref, gl_t)
    more = [gl_copy(1, rel, en) for rel in range(1, moms)]
    more += [gl_copy(2, rel, down) for rel in range(moms)]
    more += [gl_copy(0, rel, up) for rel in range(moms)]
    for copy in more:
        copy.start()
    sent += more
    gg[pl.ds(pl.multiple_of(me * rows, 16), rows), :] = gg_t[me]
    gl[1, pl.ds(me * own_k, own_k), pl.ds(0, own_e), :] = gl_t[me]

    def await_gg():
        for rel in range(1, moms):
            at = lax.rem(me + rel, moms)
            view = gg.at[pl.ds(pl.multiple_of(at * rows, 16), rows), :]
            pltpu.make_async_copy(view, view, r_gg.at[at]).wait()

    def await_gl(slot):
        for rel in range(1 if slot == 1 else 0, moms):
            at = lax.rem(me + rel, moms)
            view = gl.at[slot, pl.ds(at * own_k, own_k), pl.ds(0, own_e), :]
            pltpu.make_async_copy(view, view, r_gl.at[slot, at]).wait()

    first_part = lax.broadcasted_iota(jnp.int32, (NN, WIDE), 1) < NN

    def expand(row, rows_of, cols_of):
        hi, lo = split(row)
        out = jnp.dot(rows_of * hi, cols_of, preferred_element_type=F32)
        return out + jnp.dot(rows_of * lo, cols_of, preferred_element_type=F32)

    atom = (me * pp_n) // NB

    def block_of(m, index):
        found = der_ref[m, 0:1, :]
        for i in range(1, der_ref.shape[1]):
            found = jnp.where(index == i, der_ref[m, i : i + 1, :], found)
        return found

    lefts = [expand(block_of(m, atom), rs_ref[...], ci_ref[...]) for m in range(3)]
    cut = MAIN - NN
    for pp in range(pp_n):
        pair = me * pp_n + pp
        other = nb_ref[pair // NB, lax.rem(pair, NB)]
        for m in range(3):
            right = expand(block_of(m, other), rt_ref[...], cu_ref[...])
            both = lefts[m] * right
            top = jnp.where(first_part, both, 0.0)
            low = jnp.where(first_part, 0.0, both)
            if pp:
                low = jnp.concatenate(
                    [low[:, :MAIN], pltpu.roll(low[:, MAIN:], TAIL * pp, 1)], axis=1
                )
            for dst, a, b in zip((kr_hi, kr_lo), split(top), split(low)):
                dst[pp, m, :NN, :] = a
                dst[pp, m, NN:MAIN, :] = b[:cut]
                dst[pp, m, MAIN:, :] = jnp.zeros((128, WIDE), BF)
                dst[pp, m, MAIN + TAIL * pp : MAIN + TAIL * (pp + 1), :] = b[cut:]

    lane = lax.broadcasted_iota(jnp.int32, (own_e, 128), 1)
    row = lax.broadcasted_iota(jnp.int32, (own_e, 128), 0)
    spot = lax.rem(lane, 32)

    def ring(lo, hi, n):
        n = n % span
        if n >= 128:
            lo, hi, n = hi, lo, n - 128
        if n == 0:
            return lo, hi
        a, b = pltpu.roll(lo, n, 1), pltpu.roll(hi, n, 1)
        keep = lane >= n
        return jnp.where(keep, a, b), jnp.where(keep, b, a)

    def slide(at, index):
        lo, hi = (coef.at[at, side][pl.ds(index, own_e, stride=0), :] for side in range(2))
        a = pltpu.roll(lo, 0, 1, stride=1, stride_axis=0)
        b = pltpu.roll(hi, 0, 1, stride=1, stride_axis=0)
        keep = lane >= row
        return jnp.where(keep, a, b), jnp.where(keep, b, a)

    lines = 3 * pairs
    w_at = lax.broadcasted_iota(jnp.int32, (window_n, 128), 0)
    l_at = lax.broadcasted_iota(jnp.int32, (window_n, 128), 1)
    places = (l_at == window_n - 1 - w_at, l_at == w_at)
    for s in range(2):
        flat = ph_ref[s].reshape(momenta * lines, window_n)
        spread = jnp.dot(
            flat, jnp.where(places[s], 1.0, 0.0).astype(BF), preferred_element_type=F32
        )
        sides = [None, None]
        for q in range(momenta):
            block = (momenta - q) % momenta
            x = spread[lines * q : lines * (q + 1)]
            if block % 4:
                x = pltpu.roll(x, 32 * (block % 4), 1)
            sides[block // 4] = x if sides[block // 4] is None else sides[block // 4] + x
        for at, n in ((2 * s, (0, 1)[s]), (2 * s + 1, (span - window_n, span + 1 - window_n)[s])):
            lo, hi = ring(sides[0], sides[1], n)
            coef[at, 0] = lo
            coef[at, 1] = hi

    has_low = (en > 0).astype(F32)
    has_up = (en < ens - 1).astype(F32)
    for pp in range(pp_n):
        for m in range(3):
            index = m * pairs + me * pp_n + pp
            absorb, absorb_own = slide(0, index), slide(1, index)
            emit_own, emit = slide(2, index), slide(3, index)
            for slot in range(3):
                pick = []
                for side in range(2):
                    if slot == 0:
                        x = jnp.where(spot >= row, absorb[side] * has_low, 0.0)
                    elif slot == 1:
                        x = jnp.where(spot >= row, emit_own[side], absorb_own[side])
                    else:
                        x = jnp.where(spot <= row, emit[side] * has_up, 0.0)
                    pick.append(x)
                for k in range(0, momenta, 2):
                    even, odd = ring(*pick, 32 * k), ring(*pick, 32 * (k + 1))
                    at = m * all_rows + k * own_e
                    for side in range(2):
                        both = jnp.concatenate([even[side], odd[side]], axis=0)
                        toe[slot, pp, at : at + 2 * own_e, 128 * side : 128 * (side + 1)] = (
                            both.astype(BF)
                        )

    def of_pair(block, pp):
        return jnp.concatenate(
            [block[:, MAIN * pp : MAIN * (pp + 1)], block[:, MAIN * pp_n :]], axis=1
        )

    await_gg()
    for pp in range(pp_n):
        swapped = jnp.dot(
            of_pair(gg[...], pp), swap_ref[pp], preferred_element_type=F32
        ).astype(BF)
        for m in range(3):
            w = lax.dot_general(swapped, kr_hi[pp, m], NT, preferred_element_type=F32)
            w = w + lax.dot_general(swapped, kr_lo[pp, m], NT, preferred_element_type=F32)
            wgt[pp, m] = w.astype(BF)

    def window(slot, pp):
        g = of_pair(gl[slot].reshape(span, cols), pp)
        for m in range(3):
            t = toe[slot, pp, m * all_rows : (m + 1) * all_rows, :]
            h = jnp.dot(t, g, preferred_element_type=F32)
            if slot == 1:
                acc[pp, m] = h
            else:
                acc[pp, m] += h

    def pair_sums(slot, pp, m):
        g = of_pair(gl[slot].reshape(span, cols), pp)
        z = lax.dot_general(wgt[pp, m], g, NT, preferred_element_type=F32)
        total = None
        for k in range(4):
            a = z[own_e * k : own_e * (k + 1)]
            b = z[own_e * (k + 4) : own_e * (k + 5)]
            lo, hi = ring(a[:, :128] + b[:, 128:], a[:, 128:] + b[:, :128], span - 32 * k)
            total = (lo, hi) if total is None else (total[0] + lo, total[1] + hi)
        return total

    step = lax.broadcasted_iota(jnp.int32, (8, 128), 0)

    def diagonals(a, b):
        total = None
        for at in range(0, own_e, 8):
            x = pltpu.roll(a[at : at + 8], (127 - at) % 128, 1)
            x = x + pltpu.roll(b[at : at + 8], (127 + own_e - at) % 128, 1)
            total = x if total is None else total + x
        for bit in (1, 2, 4):
            total = jnp.where(step & bit != 0, pltpu.roll(total, 128 - bit, 1), total)
        return total

    await_gl(1)
    own_sums = {(pp, m): pair_sums(1, pp, m) for pp in range(pp_n) for m in range(3)}
    await_gl(2)
    found = []
    scale = 1.0 / (NO * np.sqrt(np.float32(momenta * ens * own_e)))
    for pp in range(pp_n):
        for m in range(3):
            above = pair_sums(2, pp, m)
            line = []
            for side in range(2):
                a = jnp.where(spot > row, own_sums[pp, m][side], 0.0)
                b = jnp.where(spot <= row, above[side] * has_up, 0.0)
                line.append(jnp.sum(diagonals(a, b), axis=0, keepdims=True) * scale)
            found.append(jnp.concatenate(line, axis=1))
    found.append(jnp.zeros((8 - len(found), span), F32))
    part[...] = jnp.concatenate(found, axis=0)
    got_z[iz] = part[...]

    def z_copy(rel):
        to = lax.rem(iz + rel, nz)
        return pltpu.make_async_remote_copy(
            src_ref=part, dst_ref=got_z.at[iz],
            send_sem=s_z.at[rel], recv_sem=r_z.at[iz],
            device_id={"mom": me, "en": (iy * nz + to) * nx + ix}, device_id_type=MESH,
        )

    z_sent = [z_copy(rel) for rel in range(1, nz)]
    for copy in z_sent:
        copy.start()

    for pp in range(pp_n):
        window(1, pp)
        window(2, pp)
    await_gl(0)
    tail = None
    for pp in range(pp_n):
        window(0, pp)
        se = None
        for m in range(3):
            hi, lo = split(acc[pp, m])
            for x, y in ((hi, kr_hi), (lo, kr_hi), (hi, kr_lo)):
                term = jnp.dot(x, y[pp, m], preferred_element_type=F32)
                se = term if se is None else se + term
        se_t[:, MAIN * pp : MAIN * (pp + 1)] = se[:, :MAIN].astype(BF)
        tail = se[:, MAIN:] if tail is None else tail + se[:, MAIN:]
    se_t[:, MAIN * pp_n :] = tail.astype(BF)

    def se_copy(rel):
        to = lax.rem(me + rel, moms)
        return pltpu.make_async_remote_copy(
            src_ref=se_t.at[pl.ds(pl.multiple_of(to * rows, 16), rows), :],
            dst_ref=se_r.at[me],
            send_sem=s_se.at[rel], recv_sem=r_se.at[me],
            device_id={"mom": to, "en": en}, device_id_type=MESH,
        )

    se_sent = [se_copy(rel) for rel in range(1, moms)]
    for copy in se_sent:
        copy.start()
    se_r[me] = se_t[pl.ds(pl.multiple_of(me * rows, 16), rows), :]

    for rel in range(1, nz):
        at = lax.rem(iz + rel, nz)
        pltpu.make_async_copy(part, got_z.at[at], r_z.at[at]).wait()
    total = got_z[0]
    for z in range(1, nz):
        total = total + got_z[z]
    plane[0] = total[:, :128]
    plane[1] = total[:, 128:]
    mine = (iy * nx + ix) * moms + me
    got_p[mine] = plane[me // 2]

    def p_copy(rel):
        om, oe, _ = plane_peer(rel)
        return pltpu.make_async_remote_copy(
            src_ref=plane.at[om // 2], dst_ref=got_p.at[mine],
            send_sem=s_p.at[rel], recv_sem=r_p.at[mine],
            device_id={"mom": om, "en": oe}, device_id_type=MESH,
        )

    @pl.loop(1, plane_n)
    def _(rel):
        p_copy(rel).start()

    for copy in sent + z_sent + se_sent:
        copy.wait_send()

    for rel in range(1, moms):
        at = lax.rem(me + rel, moms)
        pltpu.make_async_copy(se_r.at[at], se_r.at[at], r_se.at[at]).wait()

    @pl.loop(1, plane_n)
    def _(rel):
        _, _, slot = plane_peer(rel)
        pltpu.make_async_copy(got_p.at[slot], got_p.at[slot], r_p.at[slot]).wait()

    odd = lax.rem(me, 2) == 1
    for a in range(moms):
        total = got_p[a]
        for i in range(1, ny * nx):
            total = total + got_p[i * moms + a]
        pol_ref[a] = jnp.where(odd, pltpu.roll(total, 64, 1), total)

    @pl.loop(1, plane_n)
    def _(rel):
        p_copy(rel).wait_send()


def finish(se_ref, pol_ref, out_ref, pol_out, rows_f):
    own_k, own_e, pairs, _ = out_ref.shape
    moms, rows, _ = se_ref.shape
    pp_n = pairs // moms
    for a in range(moms):
        block = se_ref[a].astype(F32)
        tail = block[:, MAIN * pp_n :]
        for pp in range(pp_n):
            at = pl.ds(a * pp_n + pp, rows, stride=pairs)
            rows_f.at[0][at, :] = block[:, MAIN * pp : MAIN * pp + 128]
            rows_f.at[1][at, :] = block[:, MAIN * pp + 128 : MAIN * (pp + 1)]
            rows_f.at[2][at, :] = pltpu.roll(tail, 128 - TAIL * pp, 1) if pp else tail
    whole = jnp.concatenate([rows_f[0], rows_f[1], rows_f[2, :, :TAIL]], axis=1)
    out_ref[...] = whole.reshape(own_k, own_e, pairs, 2 * NN).astype(BF)
    own_q, _, _, window_n = pol_out.shape
    for a in range(moms):
        total = pol_ref[a]
        for q in range(own_q):
            x = pltpu.roll(total, 128 - 32 * q, 1) if q else total
            for pp in range(pp_n):
                for m in range(3):
                    line = pp * 3 + m
                    pol_out[q, m, a * pp_n + pp, :] = x[line, :window_n]


def body(green_less, green_greater, derivative, neighbours, phonon):
    own_k, own_e, pairs, width = green_less.shape
    momenta, window_n = phonon.shape[1], phonon.shape[2]
    moms, ens = lax.axis_size("mom"), lax.axis_size("en")
    nx = 2
    nz = min(8, ens // nx)
    ny = ens // (nz * nx)
    dims = (moms, ens, ny, nz, nx, own_k, own_e, pairs, momenta, window_n)
    pp_n = pairs // moms
    span = 32 * momenta
    constants = [jnp.asarray(t, BF) for t in tables(pp_n)]
    vm = pl.BlockSpec(memory_space=pltpu.VMEM)
    rows = own_k * own_e
    all_rows = momenta * own_e
    cols = MAIN * pp_n + 128
    dma = pltpu.SemaphoreType.DMA
    plane_n = ny * nx * moms
    blocks, sums = pl.pallas_call(
        functools.partial(kernel, dims),
        out_shape=(
            jax.ShapeDtypeStruct((moms, rows, cols), BF),
            jax.ShapeDtypeStruct((moms, 8, 128), F32),
        ),
        in_specs=[vm, vm, vm, pl.BlockSpec(memory_space=pltpu.SMEM)] + [vm] * 6,
        out_specs=(vm, vm),
        scratch_shapes=[
            pltpu.VMEM((3, rows * pairs, 128), F32),
            pltpu.VMEM((moms, own_k, own_e, cols), BF),
            pltpu.VMEM((moms, rows, cols), BF),
            pltpu.VMEM((3, momenta, 32, cols), BF),
            pltpu.VMEM((all_rows, cols), BF),
            pltpu.VMEM((4, 2, 3 * pairs, 128), F32),
            pltpu.VMEM((3, pp_n, 3 * all_rows, span), BF),
            pltpu.VMEM((pp_n, 3, WIDE, WIDE), BF),
            pltpu.VMEM((pp_n, 3, WIDE, WIDE), BF),
            pltpu.VMEM((pp_n, 3, all_rows, WIDE), BF),
            pltpu.VMEM((pp_n, 3, all_rows, WIDE), F32),
            pltpu.VMEM((all_rows, cols), BF),
            pltpu.VMEM((8, span), F32),
            pltpu.VMEM((nz, 8, span), F32),
            pltpu.VMEM((2, 8, 128), F32),
            pltpu.VMEM((plane_n, 8, 128), F32),
            dma((moms,)), dma((moms,)), dma((3, moms)), dma((3, moms)),
            dma((moms,)), dma((moms,)), dma((nz,)), dma((nz,)), dma((plane_n,)), dma((plane_n,)),
        ],
        compiler_params=pltpu.CompilerParams(collective_id=0, has_side_effects=True),
    )(
        green_less, green_greater, derivative.transpose(1, 0, 2), neighbours,
        phonon.transpose(0, 1, 3, 4, 2), *constants,
    )
    self_energy, pol = pl.pallas_call(
        finish,
        out_shape=(
            jax.ShapeDtypeStruct((own_k, own_e, pairs, width), BF),
            jax.ShapeDtypeStruct((momenta // moms, 3, pairs, window_n), F32),
        ),
        in_specs=[vm, vm],
        out_specs=(vm, vm),
        scratch_shapes=[pltpu.VMEM((3, rows * pairs, 128), F32)],
    )(blocks, sums)
    return self_energy, pol.transpose(0, 3, 1, 2)


def solution(mesh):
    return jax.shard_map(
        body,
        mesh=mesh,
        in_specs=(P("mom", "en", None, None), P("mom", "en", None, None), P(), P(), P()),
        out_specs=(P("mom", "en", None, None), P("mom", None, None, None)),
        check_vma=False,
    )
```

```python
import functools

import jax
import jax.numpy as jnp
import numpy as np
from jax import lax
from jax.experimental import pallas as pl
from jax.experimental.pallas import tpu as pltpu
from jax.sharding import PartitionSpec as P

NO = 12
NB = 4
NN = NO * NO
MAIN = 256
TAIL = 2 * NN - MAIN
WIDE = MAIN + 128
NX = 2
MESH = pl.DeviceIdType.MESH
BF = jnp.bfloat16
F32 = jnp.float32
NT = (((1,), (1,)), ((), ()))


def tables():
    r = np.arange(NN)
    col = np.arange(2 * NN)
    sub = col % NN
    rows_s = (r[None, :] % NO == r[:, None] // NO).astype(np.float32)
    rows_t = (r[None, :] % NO == r[:, None] % NO).astype(np.float32)
    cols_i = np.zeros((NN, WIDE), np.float32)
    cols_u = np.zeros((NN, WIDE), np.float32)
    cols_i[:, : 2 * NN] = r[:, None] // NO == sub[None, :] // NO
    cols_u[:, : 2 * NN] = r[:, None] // NO == sub[None, :] % NO
    swap = np.zeros((WIDE, WIDE), np.float32)
    flipped = (col // NN) * NN + (sub % NO) * NO + sub // NO
    swap[flipped, col] = np.where(col < NN, 1.0, -1.0)
    return rows_s, rows_t, cols_i, cols_u, swap


def split(x):
    hi = x.astype(BF)
    return hi, (x - hi.astype(F32)).astype(BF)


def kernel(
    dims,
    gl_hbm, gg_hbm, der_hbm, nb_hbm, ph_hbm, rs_hbm, rt_hbm, ci_hbm, cu_hbm, swap_hbm,
    se_ref, pol_ref,
    gl_in, gg_in, der_ref, nb_ref, ph_ref, rs_ref, rt_ref, ci_ref, cu_ref, swap_ref,
    rows_f, gl_t, gg_t, gl_r, gg_r, gl, gl_tail, gg_tail, coef, toe, kr_hi, kr_lo, wgt, acc,
    se_t, se_r, part, got_z, plane, got_p,
    loads, s_gg, r_gg, s_own, s_halo, r_gl, s_se, r_se, s_z, r_z, s_p, r_p,
):
    moms, ens, ny, nz, own_k, own_e, pairs, momenta, window_n = dims
    rows = own_k * own_e
    all_rows = momenta * own_e
    span = 32 * momenta
    groups = rows // 8
    me = lax.axis_index("mom")
    en = lax.axis_index("en")
    ring, ix = en // NX, en % NX
    iy, iz = ring // nz, ring % nz
    rings = ens // NX
    above_ring, below_ring = lax.rem(ring + 1, rings), lax.rem(ring + rings - 1, rings)
    pair = me * NX + ix

    hbm = (gg_hbm, gl_hbm, ph_hbm, der_hbm, nb_hbm, rs_hbm, rt_hbm, ci_hbm, cu_hbm, swap_hbm)
    near = (gg_in, gl_in, ph_ref, der_ref, nb_ref, rs_ref, rt_ref, ci_ref, cu_ref, swap_ref)
    fetch = [pltpu.make_async_copy(a, b, loads.at[i]) for i, (a, b) in enumerate(zip(hbm, near))]
    for copy in fetch:
        copy.start()

    barrier = pltpu.get_barrier_semaphore()

    def greet(mom_at, en_at):
        pl.semaphore_signal(
            barrier, inc=1, device_id={"mom": mom_at, "en": en_at}, device_id_type=MESH
        )

    mom_of = [me] + [lax.rem(me + rel, moms) for rel in range(1, moms)]
    ix_of = [ix, 1 - ix]
    mates = [(rx, rm) for rx in range(NX) for rm in range(moms)]
    for rx, rm in mates:
        if rx or rm:
            greet(mom_of[rm], ring * NX + ix_of[rx])
        greet(mom_of[rm], above_ring * NX + ix_of[rx])
        greet(mom_of[rm], below_ring * NX + ix_of[rx])
    z_of = [(iy * nz + lax.rem(iz + rel, nz)) * NX + ix for rel in range(nz)]
    for rel in range(1, nz):
        greet(me, z_of[rel])
    y_of = [lax.rem(iy + ry, ny) for ry in range(ny)]
    flats = [(ry, rx, rm) for ry in range(ny) for rx in range(NX) for rm in range(moms)][1:]
    for ry, rx, rm in flats:
        if ry:
            greet(mom_of[rm], (y_of[ry] * nz + iz) * NX + ix_of[rx])
    greeted = 3 * len(mates) - 1 + nz - 1 + (ny - 1) * len(mates)

    lane8 = lax.broadcasted_iota(jnp.int32, (8, 128), 1)

    def pack_tail(x):
        halves = [jnp.zeros((8, 128), F32), jnp.zeros((8, 128), F32)]
        for g in range(groups):
            y = x[8 * g : 8 * (g + 1)]
            at = TAIL * (g % 4)
            y = pltpu.roll(y, at, 1) if at else y
            keep = (lane8 >= at) & (lane8 < at + TAIL)
            halves[g // 4] = jnp.where(keep, y, halves[g // 4])
        return jnp.concatenate(halves, axis=1)

    def unpack_tail(x):
        found = []
        for g in range(groups):
            y = x[:, 128 * (g // 4) : 128 * (g // 4 + 1)]
            at = TAIL * (g % 4)
            y = pltpu.roll(y, 128 - at, 1) if at else y
            found.append(jnp.where(lane8 < TAIL, y, 0.0))
        return found

    def by_pair(src, dst):
        whole = src[...].astype(F32).reshape(rows * pairs, 2 * NN)
        rows_f[0] = whole[:, :128]
        rows_f[1] = whole[:, 128:MAIN]
        rows_f[2, :, :TAIL] = whole[:, MAIN:]
        for p in range(pairs):
            x = [rows_f.at[c][pl.ds(p, rows, stride=pairs), :] for c in range(3)]
            dst[p, :rows, :128] = x[0].astype(BF)
            dst[p, :rows, 128:] = x[1].astype(BF)
            dst[p, rows:, :] = pack_tail(x[2]).astype(BF)

    def remote(src, dst, send, recv, mom_at, en_at):
        return pltpu.make_async_remote_copy(
            src_ref=src, dst_ref=dst, send_sem=send, recv_sem=recv,
            device_id={"mom": mom_at, "en": en_at}, device_id_type=MESH,
        )

    def landed(ref, sem):
        pltpu.make_async_copy(ref, ref, sem).wait()

    sent = []

    def send(copy):
        copy.start()
        sent.append(copy)

    fetch[0].wait()
    by_pair(gg_in, gg_t)
    pl.semaphore_wait(barrier, greeted)
    for i, (rx, rm) in enumerate(mates):
        if i:
            to = mom_of[rm] * NX + ix_of[rx]
            send(remote(
                gg_t.at[to], gg_r.at[ix, me], s_gg.at[i], r_gg.at[ix, me],
                mom_of[rm], ring * NX + ix_of[rx],
            ))
    fetch[1].wait()
    by_pair(gl_in, gl_t)
    for i, (rx, rm) in enumerate(mates):
        if i:
            to = mom_of[rm] * NX + ix_of[rx]
            send(remote(
                gl_t.at[to], gl_r.at[1 + ix, me], s_own.at[i], r_gl.at[1 + ix, me],
                mom_of[rm], ring * NX + ix_of[rx],
            ))
    slot = 3 - 3 * ix
    other_ring = lax.rem(ring + rings + 2 * ix - 1, rings)
    for i, (rx, rm) in enumerate(mates):
        to = mom_of[rm] * NX + ix_of[rx]
        send(remote(
            gl_t.at[to], gl_r.at[slot, me], s_halo.at[i], r_gl.at[slot, me],
            mom_of[rm], other_ring * NX + ix_of[rx],
        ))
    gg_r[ix, me] = gg_t[pair]
    gl_r[1 + ix, me] = gl_t[pair]

    def await_ring(buffer, first, sems):
        for i, (rx, rm) in enumerate(mates):
            if i:
                at = first + ix_of[rx]
                landed(buffer.at[at, mom_of[rm]], sems.at[at, mom_of[rm]])

    gl[:, :, own_e:, :] = jnp.zeros((4, momenta, 32 - own_e, MAIN), BF)
    gl_tail[:, :, own_e:, :] = jnp.zeros((4, momenta, 32 - own_e, 128), BF)

    for copy in fetch[2:]:
        copy.wait()

    first_part = lax.broadcasted_iota(jnp.int32, (NN, WIDE), 1) < NN

    def expand(row, rows_of, cols_of):
        hi, lo = split(row)
        out = jnp.dot(rows_of * hi, cols_of, preferred_element_type=F32)
        return out + jnp.dot(rows_of * lo, cols_of, preferred_element_type=F32)

    def block_of(m, index):
        found = der_ref[m, 0:1, :]
        for i in range(1, der_ref.shape[1]):
            found = jnp.where(index == i, der_ref[m, i : i + 1, :], found)
        return found

    cut = MAIN - NN
    other = nb_ref[pair // NB, lax.rem(pair, NB)]
    for m in range(3):
        left = expand(block_of(m, pair // NB), rs_ref[...], ci_ref[...])
        right = expand(block_of(m, other), rt_ref[...], cu_ref[...])
        both = left * right
        top = jnp.where(first_part, both, 0.0)
        low = jnp.where(first_part, 0.0, both)
        for dst, a, b in zip((kr_hi, kr_lo), split(top), split(low)):
            dst[m, :NN, :] = a
            dst[m, NN : 2 * NN, :] = b
            dst[m, 2 * NN :, :] = jnp.zeros((WIDE - 2 * NN, WIDE), BF)

    lane = lax.broadcasted_iota(jnp.int32, (own_e, 128), 1)
    row = lax.broadcasted_iota(jnp.int32, (own_e, 128), 0)
    spot = lax.rem(lane, 32)

    def turn(lo, hi, n):
        n = n % span
        if n >= 128:
            lo, hi, n = hi, lo, n - 128
        if n == 0:
            return lo, hi
        a, b = pltpu.roll(lo, n, 1), pltpu.roll(hi, n, 1)
        keep = lane >= n
        return jnp.where(keep, a, b), jnp.where(keep, b, a)

    def slide(at, index):
        lo, hi = (coef.at[at, side][pl.ds(index, own_e, stride=0), :] for side in range(2))
        a = pltpu.roll(lo, 0, 1, stride=1, stride_axis=0)
        b = pltpu.roll(hi, 0, 1, stride=1, stride_axis=0)
        keep = lane >= row
        return jnp.where(keep, a, b), jnp.where(keep, b, a)

    lines = 3 * pairs
    w_at = lax.broadcasted_iota(jnp.int32, (window_n, 128), 0)
    l_at = lax.broadcasted_iota(jnp.int32, (window_n, 128), 1)
    places = (l_at == window_n - 1 - w_at, l_at == w_at)
    for s in range(2):
        flat = ph_ref[s].reshape(momenta * lines, window_n)
        spread = jnp.dot(
            flat, jnp.where(places[s], 1.0, 0.0).astype(BF), preferred_element_type=F32
        )
        sides = [None, None]
        for q in range(momenta):
            block = (momenta - q) % momenta
            x = spread[lines * q : lines * (q + 1)]
            if block % 4:
                x = pltpu.roll(x, 32 * (block % 4), 1)
            sides[block // 4] = x if sides[block // 4] is None else sides[block // 4] + x
        for at, n in ((2 * s, (0, 1)[s]), (2 * s + 1, (span - window_n, span + 1 - window_n)[s])):
            lo, hi = turn(sides[0], sides[1], n)
            coef[at, 0] = lo
            coef[at, 1] = hi

    for m in range(3):
        index = m * pairs + pair
        absorb, absorb_own = slide(0, index), slide(1, index)
        emit_own, emit = slide(2, index), slide(3, index)
        for step in range(3):
            pick = []
            for side in range(2):
                if step == 0:
                    x = jnp.where(spot >= row, absorb[side], 0.0)
                elif step == 1:
                    x = jnp.where(spot >= row, emit_own[side], absorb_own[side])
                else:
                    x = jnp.where(spot <= row, emit[side], 0.0)
                pick.append(x)
            for k in range(0, momenta, 2):
                even, odd = turn(*pick, 32 * k), turn(*pick, 32 * (k + 1))
                at = m * all_rows + k * own_e
                for side in range(2):
                    both = jnp.concatenate([even[side], odd[side]], axis=0)
                    toe[step, at : at + 2 * own_e, 128 * side : 128 * (side + 1)] = both.astype(BF)

    has_low = (ring > 0).astype(F32)
    has_up = (ring < rings - 1).astype(F32)

    await_ring(gg_r, 0, r_gg)
    for i in range(NX):
        for a in range(moms):
            tails = unpack_tail(gg_r[i, a, rows:, :].astype(F32))
            gg_tail[i, rows * a : rows * (a + 1), :] = jnp.concatenate(tails, axis=0).astype(BF)
        block = jnp.concatenate(
            [gg_r[i, :, :rows, :].reshape(all_rows, MAIN), gg_tail[i]], axis=1
        )
        swapped = jnp.dot(block, swap_ref[...], preferred_element_type=F32).astype(BF)
        for m in range(3):
            w = lax.dot_general(swapped, kr_hi[m], NT, preferred_element_type=F32)
            w = w + lax.dot_general(swapped, kr_lo[m], NT, preferred_element_type=F32)
            wgt[i, m] = w.astype(BF)

    def spread_rows(j):
        for a in range(moms):
            for k in range(own_k):
                gl[j, own_k * a + k, :own_e, :] = gl_r[j, a, own_e * k : own_e * (k + 1), :]
            tails = unpack_tail(gl_r[j, a, rows:, :].astype(F32))
            for k in range(own_k):
                x = jnp.concatenate(tails[3 * k : 3 * (k + 1)], axis=0)
                gl_tail[j, own_k * a + k, :own_e, :] = x.astype(BF)

    def block_at(j):
        return jnp.concatenate(
            [gl[j].reshape(span, MAIN), gl_tail[j].reshape(span, 128)], axis=1
        )

    def window(i, step):
        g = block_at(i + step)
        for m in range(3):
            t = toe[step, m * all_rows : (m + 1) * all_rows, :]
            h = jnp.dot(t, g, preferred_element_type=F32)
            if (i, step) == (0, 0):
                h = h * has_low
            if (i, step) == (NX - 1, 2):
                h = h * has_up
            if step == 1:
                acc[i, m] = h
            else:
                acc[i, m] += h

    def pair_sums(i, j, m):
        z = lax.dot_general(wgt[i, m], block_at(j), NT, preferred_element_type=F32)
        total = None
        for k in range(4):
            a = z[own_e * k : own_e * (k + 1)]
            b = z[own_e * (k + 4) : own_e * (k + 5)]
            lo, hi = turn(a[:, :128] + b[:, 128:], a[:, 128:] + b[:, :128], span - 32 * k)
            total = (lo, hi) if total is None else (total[0] + lo, total[1] + hi)
        return total

    row8 = lax.broadcasted_iota(jnp.int32, (8, 128), 0)

    def diagonals(a, b):
        total = None
        for at in range(0, own_e, 8):
            x = pltpu.roll(a[at : at + 8], (127 - at) % 128, 1)
            x = x + pltpu.roll(b[at : at + 8], (127 + own_e - at) % 128, 1)
            total = x if total is None else total + x
        for bit in (1, 2, 4):
            total = jnp.where(row8 & bit != 0, pltpu.roll(total, 128 - bit, 1), total)
        return total

    await_ring(gl_r, 1, r_gl)
    spread_rows(1)
    spread_rows(2)
    own_sums, up_sums = [], []
    for m in range(3):
        x, y = pair_sums(0, 1, m), pair_sums(1, 2, m)
        own_sums.append([x[side] + y[side] for side in range(2)])
        up_sums.append(pair_sums(0, 2, m))
    for a in range(moms):
        landed(gl_r.at[3, a], r_gl.at[3, a])
    spread_rows(3)
    scale = 1.0 / (NO * np.sqrt(np.float32(momenta * ens * own_e)))
    found = [[], []]
    for m in range(3):
        last = pair_sums(1, 3, m)
        for side in range(2):
            a = jnp.where(spot > row, own_sums[m][side], 0.0)
            b = jnp.where(spot <= row, up_sums[m][side] + last[side] * has_up, 0.0)
            found[side].append(jnp.sum(diagonals(a, b), axis=0, keepdims=True) * scale)
    part[...] = jnp.concatenate(found[0] + found[1] + [jnp.zeros((2, 128), F32)], axis=0)
    got_z[iz] = part[...]
    for rel in range(1, nz):
        send(remote(part, got_z.at[iz], s_z.at[rel], r_z.at[iz], me, z_of[rel]))

    window(0, 1)
    window(1, 1)
    window(0, 2)
    window(1, 0)
    window(1, 2)
    for a in range(moms):
        landed(gl_r.at[0, a], r_gl.at[0, a])
    spread_rows(0)
    window(0, 0)
    for i in range(NX):
        se = None
        for m in range(3):
            hi, lo = split(acc[i, m])
            for x, y in ((hi, kr_hi), (lo, kr_hi), (hi, kr_lo)):
                term = jnp.dot(x, y[m], preferred_element_type=F32)
                se = term if se is None else se + term
        for a in range(moms):
            x = se[rows * a : rows * (a + 1)]
            se_t[i, a, :rows, :] = x[:, :MAIN].astype(BF)
            se_t[i, a, rows:, :] = pack_tail(x[:, MAIN:]).astype(BF)
    for i, (rx, rm) in enumerate(mates):
        if i:
            send(remote(
                se_t.at[ix_of[rx], mom_of[rm]], se_r.at[pair], s_se.at[i], r_se.at[pair],
                mom_of[rm], ring * NX + ix_of[rx],
            ))
    se_r[pair] = se_t[ix, me]

    for rel in range(1, nz):
        at = lax.rem(iz + rel, nz)
        landed(got_z.at[at], r_z.at[at])
    total = got_z[0]
    for z in range(1, nz):
        total = total + got_z[z]
    plane[...] = total
    got_p[iy, pair] = total
    for i, (ry, rx, rm) in enumerate(flats):
        send(remote(
            plane, got_p.at[iy, pair], s_p.at[i], r_p.at[iy, pair],
            mom_of[rm], (y_of[ry] * nz + iz) * NX + ix_of[rx],
        ))

    for i, (rx, rm) in enumerate(mates):
        if i:
            at = mom_of[rm] * NX + ix_of[rx]
            landed(se_r.at[at], r_se.at[at])
    for p in range(pairs):
        at = pl.ds(p, rows, stride=pairs)
        rows_f.at[0][at, :] = se_r[p, :rows, :128].astype(F32)
        rows_f.at[1][at, :] = se_r[p, :rows, 128:].astype(F32)
        tails = unpack_tail(se_r[p, rows:, :].astype(F32))
        rows_f.at[2][at, :] = jnp.concatenate(tails, axis=0)
    whole = jnp.concatenate([rows_f[0], rows_f[1], rows_f[2, :, :TAIL]], axis=1)
    se_ref[...] = whole.reshape(own_k, own_e, pairs, 2 * NN).astype(BF)

    for ry, rx, rm in flats:
        at = (y_of[ry], mom_of[rm] * NX + ix_of[rx])
        landed(got_p.at[at[0], at[1]], r_p.at[at[0], at[1]])
    own_q = momenta // moms
    for p in range(pairs):
        total = got_p[0, p]
        for y in range(1, ny):
            total = total + got_p[y, p]
        x = jnp.where(me >= moms // 2, total[3:6], total[0:3])
        x = jnp.where(lax.rem(me, 2) == 1, pltpu.roll(x, 64, 1), x)
        for q in range(own_q):
            y = pltpu.roll(x, 128 - 32 * q, 1) if q else x
            for m in range(3):
                pol_ref[q, m, p, :] = y[m, :window_n]
    for copy in sent:
        copy.wait_send()


def deliver(se_ref, pol_ref, se_out, pol_out, sems):
    copies = [
        pltpu.make_async_copy(se_ref, se_out, sems.at[0]),
        pltpu.make_async_copy(pol_ref, pol_out, sems.at[1]),
    ]
    for copy in copies:
        copy.start()
    for copy in copies:
        copy.wait()


def body(green_less, green_greater, derivative, neighbours, phonon):
    own_k, own_e, pairs, width = green_less.shape
    momenta, window_n = phonon.shape[1], phonon.shape[2]
    moms, ens = lax.axis_size("mom"), lax.axis_size("en")
    nz = min(8, ens // NX)
    ny = ens // (nz * NX)
    dims = (moms, ens, ny, nz, own_k, own_e, pairs, momenta, window_n)
    mates = moms * NX
    span = 32 * momenta
    rows = own_k * own_e
    all_rows = momenta * own_e
    sent = rows + 8
    constants = [jnp.asarray(t, BF) for t in tables()]
    dma = pltpu.SemaphoreType.DMA
    operands = [
        green_less, green_greater, derivative.transpose(1, 0, 2), neighbours,
        phonon.transpose(0, 1, 3, 4, 2), *constants,
    ]
    order = [0, 1, 2, 4, 5, 6, 7, 8, 9]
    near = [pltpu.VMEM(operands[i].shape, operands[i].dtype) for i in order]
    near.insert(3, pltpu.SMEM(neighbours.shape, neighbours.dtype))
    self_energy, pol = pl.pallas_call(
        functools.partial(kernel, dims),
        out_shape=(
            pltpu.VMEM((own_k, own_e, pairs, width), BF),
            pltpu.VMEM((momenta // moms, 3, pairs, window_n), F32),
        ),
        in_specs=[pl.BlockSpec(memory_space=pl.ANY)] * len(operands),
        out_specs=(pl.BlockSpec(memory_space=pltpu.VMEM),) * 2,
        scratch_shapes=near + [
            pltpu.VMEM((3, rows * pairs, 128), F32),
            pltpu.VMEM((pairs, sent, MAIN), BF),
            pltpu.VMEM((pairs, sent, MAIN), BF),
            pltpu.VMEM((4, moms, sent, MAIN), BF),
            pltpu.VMEM((NX, moms, sent, MAIN), BF),
            pltpu.VMEM((4, momenta, 32, MAIN), BF),
            pltpu.VMEM((4, momenta, 32, 128), BF),
            pltpu.VMEM((NX, all_rows, 128), BF),
            pltpu.VMEM((4, 2, 3 * pairs, 128), F32),
            pltpu.VMEM((3, 3 * all_rows, span), BF),
            pltpu.VMEM((3, WIDE, WIDE), BF),
            pltpu.VMEM((3, WIDE, WIDE), BF),
            pltpu.VMEM((NX, 3, all_rows, WIDE), BF),
            pltpu.VMEM((NX, 3, all_rows, WIDE), F32),
            pltpu.VMEM((NX, moms, sent, MAIN), BF),
            pltpu.VMEM((pairs, sent, MAIN), BF),
            pltpu.VMEM((8, 128), F32),
            pltpu.VMEM((nz, 8, 128), F32),
            pltpu.VMEM((8, 128), F32),
            pltpu.VMEM((ny, pairs, 8, 128), F32),
            dma((len(operands),)), dma((mates,)), dma((NX, moms)), dma((mates,)), dma((mates,)),
            dma((4, moms)), dma((mates,)), dma((pairs,)), dma((nz,)), dma((nz,)),
            dma((ny * mates,)), dma((ny, pairs)),
        ],
        compiler_params=pltpu.CompilerParams(collective_id=0, has_side_effects=True),
    )(*operands)
    self_energy = pltpu.with_memory_space_constraint(self_energy, pltpu.VMEM)
    pol = pltpu.with_memory_space_constraint(pol, pltpu.VMEM)
    self_energy, pol = pl.pallas_call(
        deliver,
        out_shape=tuple(jax.ShapeDtypeStruct(x.shape, x.dtype) for x in (self_energy, pol)),
        in_specs=[pl.BlockSpec(memory_space=pltpu.VMEM)] * 2,
        out_specs=(pl.BlockSpec(memory_space=pl.ANY),) * 2,
        scratch_shapes=[dma((2,))],
        compiler_params=pltpu.CompilerParams(vmem_limit_bytes=16 << 20),
    )(self_energy, pol)
    return self_energy, pol.transpose(0, 3, 1, 2)


def solution(mesh):
    return jax.shard_map(
        body,
        mesh=mesh,
        in_specs=(P("mom", "en", None, None), P("mom", "en", None, None), P(), P(), P()),
        out_specs=(P("mom", "en", None, None), P("mom", None, None, None)),
        check_vma=False,
    )
```

```python
import functools

import jax
import jax.numpy as jnp
import numpy as np
from jax import lax
from jax.experimental import pallas as pl
from jax.experimental.pallas import tpu as pltpu
from jax.sharding import PartitionSpec as P

NO = 12
NB = 4
NN = NO * NO
MAIN = 256
TAIL = 2 * NN - MAIN
WIDE = MAIN + 128
NX = 2
MESH = pl.DeviceIdType.MESH
BF = jnp.bfloat16
F32 = jnp.float32
NT = (((1,), (1,)), ((), ()))


def tables():
    r = np.arange(NN)
    first, second = r // NO, r % NO
    rows = np.zeros((4, NN, NN), np.float32)
    cols = np.zeros((4, NN, WIDE), np.float32)
    sub = np.arange(2 * NN) % NN
    for at, (of_row, own, of_col, other) in enumerate((
        (second, first, first, sub // NO),
        (second, second, first, sub % NO),
        (first, second, second, sub // NO),
        (first, first, second, sub % NO),
    )):
        rows[at] = of_row[None, :] == own[:, None]
        cols[at, :, : 2 * NN] = of_col[:, None] == other[None, :]
    return rows, cols


def split(x):
    hi = x.astype(BF)
    return hi, (x - hi.astype(F32)).astype(BF)


def kernel(
    dims,
    gl_hbm, gg_hbm, der_hbm, nb_hbm, ph_hbm, rt_hbm, ct_hbm,
    se_ref, pol_ref,
    gl_in, gg_in, der_ref, nb_ref, ph_ref, rt_ref, ct_ref,
    rows_f, gl_t, gg_t, gl_r, gg_r, gl, gl_tail, gg_tail, coef, toe, ks_hi, ks_lo, ks_tail, kw,
    wgt, wgt_tail, acc, acc_tail,
    se_t, se_r, part, got_z, plane, got_p,
    loads, s_gg, r_gg, s_own, s_halo, r_gl, s_se, r_se, s_z, r_z, s_p, r_p,
):
    moms, ens, ny, nz, own_k, own_e, pairs, momenta, window_n = dims
    rows = own_k * own_e
    all_rows = momenta * own_e
    span = 32 * momenta
    groups = rows // 8
    me = lax.axis_index("mom")
    en = lax.axis_index("en")
    ring, ix = en // NX, en % NX
    iy, iz = ring // nz, ring % nz
    rings = ens // NX
    above_ring, below_ring = lax.rem(ring + 1, rings), lax.rem(ring + rings - 1, rings)
    pair = me * NX + ix

    hbm = (gg_hbm, gl_hbm, ph_hbm, der_hbm, nb_hbm, rt_hbm, ct_hbm)
    near = (gg_in, gl_in, ph_ref, der_ref, nb_ref, rt_ref, ct_ref)
    fetch = [pltpu.make_async_copy(a, b, loads.at[i]) for i, (a, b) in enumerate(zip(hbm, near))]
    for copy in fetch:
        copy.start()

    barrier = pltpu.get_barrier_semaphore()

    def greet(mom_at, en_at):
        pl.semaphore_signal(
            barrier, inc=1, device_id={"mom": mom_at, "en": en_at}, device_id_type=MESH
        )

    mom_of = [me] + [lax.rem(me + rel, moms) for rel in range(1, moms)]
    ix_of = [ix, 1 - ix]
    mates = [(rx, rm) for rx in range(NX) for rm in range(moms)]
    for rx, rm in mates:
        if rx or rm:
            greet(mom_of[rm], ring * NX + ix_of[rx])
        greet(mom_of[rm], above_ring * NX + ix_of[rx])
        greet(mom_of[rm], below_ring * NX + ix_of[rx])
    z_of = [(iy * nz + lax.rem(iz + rel, nz)) * NX + ix for rel in range(nz)]
    for rel in range(1, nz):
        greet(me, z_of[rel])
    y_of = [lax.rem(iy + ry, ny) for ry in range(ny)]
    flats = [(ry, rx, rm) for ry in range(ny) for rx in range(NX) for rm in range(moms)][1:]
    for ry, rx, rm in flats:
        if ry:
            greet(mom_of[rm], (y_of[ry] * nz + iz) * NX + ix_of[rx])
    greeted = 3 * len(mates) - 1 + nz - 1 + (ny - 1) * len(mates)

    lane8 = lax.broadcasted_iota(jnp.int32, (8, 128), 1)

    def pack_tail(x):
        halves = [jnp.zeros((8, 128), F32), jnp.zeros((8, 128), F32)]
        for g in range(groups):
            y = x[8 * g : 8 * (g + 1)]
            at = TAIL * (g % 4)
            y = pltpu.roll(y, at, 1) if at else y
            keep = (lane8 >= at) & (lane8 < at + TAIL)
            halves[g // 4] = jnp.where(keep, y, halves[g // 4])
        return jnp.concatenate(halves, axis=1)

    def unpack_tail(x):
        found = []
        for g in range(groups):
            y = x[:, 128 * (g // 4) : 128 * (g // 4 + 1)]
            at = TAIL * (g % 4)
            y = pltpu.roll(y, 128 - at, 1) if at else y
            found.append(jnp.where(lane8 < TAIL, y, 0.0))
        return found

    def by_pair(src, dst):
        whole = src[...].astype(F32).reshape(rows * pairs, 2 * NN)
        rows_f[0] = whole[:, :128]
        rows_f[1] = whole[:, 128:MAIN]
        rows_f[2, :, :TAIL] = whole[:, MAIN:]
        for p in range(pairs):
            x = [rows_f.at[c][pl.ds(p, rows, stride=pairs), :] for c in range(3)]
            dst[p, :rows, :128] = x[0].astype(BF)
            dst[p, :rows, 128:] = x[1].astype(BF)
            dst[p, rows:, :] = pack_tail(x[2]).astype(BF)

    def remote(src, dst, send, recv, mom_at, en_at):
        return pltpu.make_async_remote_copy(
            src_ref=src, dst_ref=dst, send_sem=send, recv_sem=recv,
            device_id={"mom": mom_at, "en": en_at}, device_id_type=MESH,
        )

    def landed(ref, sem):
        pltpu.make_async_copy(ref, ref, sem).wait()

    sent = []

    def send(copy):
        copy.start()
        sent.append(copy)

    fetch[0].wait()
    by_pair(gg_in, gg_t)
    pl.semaphore_wait(barrier, greeted)
    for i, (rx, rm) in enumerate(mates):
        if i:
            to = mom_of[rm] * NX + ix_of[rx]
            send(remote(
                gg_t.at[to], gg_r.at[ix, me], s_gg.at[i], r_gg.at[ix, me],
                mom_of[rm], ring * NX + ix_of[rx],
            ))
    fetch[1].wait()
    by_pair(gl_in, gl_t)
    for i, (rx, rm) in enumerate(mates):
        if i:
            to = mom_of[rm] * NX + ix_of[rx]
            send(remote(
                gl_t.at[to], gl_r.at[1 + ix, me], s_own.at[i], r_gl.at[1 + ix, me],
                mom_of[rm], ring * NX + ix_of[rx],
            ))
    slot = 3 - 3 * ix
    other_ring = lax.rem(ring + rings + 2 * ix - 1, rings)
    for i, (rx, rm) in enumerate(mates):
        to = mom_of[rm] * NX + ix_of[rx]
        send(remote(
            gl_t.at[to], gl_r.at[slot, me], s_halo.at[i], r_gl.at[slot, me],
            mom_of[rm], other_ring * NX + ix_of[rx],
        ))
    gg_r[ix, me] = gg_t[pair]
    gl_r[1 + ix, me] = gl_t[pair]

    def await_ring(buffer, first, sems):
        for i, (rx, rm) in enumerate(mates):
            if i:
                at = first + ix_of[rx]
                landed(buffer.at[at, mom_of[rm]], sems.at[at, mom_of[rm]])

    gl[:, :, own_e:, :] = jnp.zeros((4, momenta, 32 - own_e, MAIN), BF)
    gl_tail[...] = jnp.zeros((3, momenta, 32, 128), BF)

    for copy in fetch[2:]:
        copy.wait()

    first_part = lax.broadcasted_iota(jnp.int32, (NN, WIDE), 1) < NN
    pair_lane = lax.broadcasted_iota(jnp.int32, (NN, 128), 1)

    def expand(row, rows_of, cols_of):
        hi, lo = split(row)
        out = jnp.dot(rows_of * hi, cols_of, preferred_element_type=F32)
        return out + jnp.dot(rows_of * lo, cols_of, preferred_element_type=F32)

    def block_of(m, index):
        found = der_ref[m, 0:1, :]
        for i in range(1, der_ref.shape[1]):
            found = jnp.where(index == i, der_ref[m, i : i + 1, :], found)
        return found

    cut = MAIN - NN
    other = nb_ref[pair // NB, lax.rem(pair, NB)]
    main = 3 * MAIN
    ks_hi[main + 3 * TAIL :, :] = jnp.zeros((128 - 3 * TAIL, MAIN), BF)
    ks_lo[main + 3 * TAIL :, :] = jnp.zeros((128 - 3 * TAIL, MAIN), BF)
    ks_tail[...] = jnp.zeros((main + 128, 128), BF)
    kw[2 * MAIN :, :] = jnp.zeros((128, main + 128), BF)
    kw[:, main + 96 :] = jnp.zeros((2 * MAIN + 128, 32), BF)
    for m in range(3):
        left, right = block_of(m, pair // NB), block_of(m, other)
        both = expand(left, rt_ref[0], ct_ref[0]) * expand(right, rt_ref[1], ct_ref[1])
        tops = split(jnp.where(first_part, both, 0.0))
        lows = split(jnp.where(first_part, 0.0, both))
        at = MAIN * m
        tail_at = main + TAIL * m
        for dst, top, low in zip((ks_hi, ks_lo), tops, lows):
            dst[at : at + NN, :] = top[:, :MAIN]
            dst[at + NN : at + MAIN, :] = low[:cut, :MAIN]
            dst[tail_at : tail_at + TAIL, :] = low[cut:, :MAIN]
        last = jnp.where(first_part, 0.0, both)[:, MAIN:]
        hi = last.astype(BF).astype(F32)
        last = jnp.where(pair_lane < TAIL, hi, pltpu.roll(last - hi, TAIL, 1)).astype(BF)
        ks_tail[at + NN : at + MAIN, :] = last[:cut]
        ks_tail[tail_at : tail_at + TAIL, :] = last[cut:]
        both = expand(left, rt_ref[2], ct_ref[2]) * expand(right, rt_ref[3], ct_ref[3])
        top = jnp.where(first_part, both, 0.0)
        low = jnp.where(first_part, 0.0, -both)
        shift = lambda x: pltpu.roll(x[:, MAIN:], TAIL * m, 1) if m else x[:, MAIN:]
        lane_at = slice(main + TAIL * m, main + TAIL * (m + 1))
        last = split(shift(low))
        for half, (x, y, z) in enumerate(zip(split(top), split(low), last)):
            z = z[:, TAIL * m : TAIL * (m + 1)]
            row_at, rest = MAIN * half, 2 * MAIN + TAIL * half
            kw[row_at : row_at + NN, at : at + MAIN] = x[:, :MAIN]
            kw[row_at + NN : row_at + MAIN, at : at + MAIN] = y[:cut, :MAIN]
            kw[rest : rest + TAIL, at : at + MAIN] = y[cut:, :MAIN]
            kw[row_at : row_at + NN, lane_at] = jnp.zeros((NN, TAIL), BF)
            kw[row_at + NN : row_at + MAIN, lane_at] = z[:cut]
            kw[rest : rest + TAIL, lane_at] = z[cut:]

    lane = lax.broadcasted_iota(jnp.int32, (own_e, 128), 1)
    row = lax.broadcasted_iota(jnp.int32, (own_e, 128), 0)
    spot = lax.rem(lane, 32)

    def turn(lo, hi, n):
        n = n % span
        if n >= 128:
            lo, hi, n = hi, lo, n - 128
        if n == 0:
            return lo, hi
        a, b = pltpu.roll(lo, n, 1), pltpu.roll(hi, n, 1)
        keep = lane >= n
        return jnp.where(keep, a, b), jnp.where(keep, b, a)

    def slide(at, index):
        lo, hi = (coef.at[at, side][pl.ds(index, own_e, stride=0), :] for side in range(2))
        a = pltpu.roll(lo, 0, 1, stride=1, stride_axis=0)
        b = pltpu.roll(hi, 0, 1, stride=1, stride_axis=0)
        keep = lane >= row
        return jnp.where(keep, a, b), jnp.where(keep, b, a)

    lines = 3 * pairs
    w_at = lax.broadcasted_iota(jnp.int32, (window_n, 128), 0)
    l_at = lax.broadcasted_iota(jnp.int32, (window_n, 128), 1)
    places = (l_at == window_n - 1 - w_at, l_at == w_at)
    for s in range(2):
        flat = ph_ref[s].reshape(momenta * lines, window_n)
        spread = jnp.dot(
            flat, jnp.where(places[s], 1.0, 0.0).astype(BF), preferred_element_type=F32
        )
        sides = [None, None]
        for q in range(momenta):
            block = (momenta - q) % momenta
            x = spread[lines * q : lines * (q + 1)]
            if block % 4:
                x = pltpu.roll(x, 32 * (block % 4), 1)
            sides[block // 4] = x if sides[block // 4] is None else sides[block // 4] + x
        for at, n in ((2 * s, (0, 1)[s]), (2 * s + 1, (span - window_n, span + 1 - window_n)[s])):
            lo, hi = turn(sides[0], sides[1], n)
            coef[at, 0] = lo
            coef[at, 1] = hi

    for m in range(3):
        index = m * pairs + pair
        absorb, absorb_own = slide(0, index), slide(1, index)
        emit_own, emit = slide(2, index), slide(3, index)
        for step in range(3):
            pick = []
            for side in range(2):
                if step == 0:
                    x = jnp.where(spot >= row, absorb[side], 0.0)
                elif step == 1:
                    x = jnp.where(spot >= row, emit_own[side], absorb_own[side])
                else:
                    x = jnp.where(spot <= row, emit[side], 0.0)
                pick.append(x)
            for k in range(0, momenta, 2):
                even, odd = turn(*pick, 32 * k), turn(*pick, 32 * (k + 1))
                at = m * all_rows + k * own_e
                for side in range(2):
                    both = jnp.concatenate([even[side], odd[side]], axis=0)
                    toe[step, at : at + 2 * own_e, 128 * side : 128 * (side + 1)] = both.astype(BF)

    has_low = (ring > 0).astype(F32)
    has_up = (ring < rings - 1).astype(F32)
    tail_lane = lax.broadcasted_iota(jnp.int32, (all_rows, 128), 1)

    def moved(x, source, target):
        n = (target - source) % 128
        x = pltpu.roll(x, n, 1) if n else x
        return jnp.where((tail_lane >= target) & (tail_lane < target + TAIL), x, 0.0)

    await_ring(gg_r, 0, r_gg)
    for i in range(NX):
        for a in range(moms):
            tails = unpack_tail(gg_r[i, a, rows:, :].astype(F32))
            tails = [x + pltpu.roll(x, TAIL, 1) for x in tails]
            gg_tail[i, rows * a : rows * (a + 1), :] = jnp.concatenate(tails, axis=0).astype(BF)
        block = gg_r[i, :, :rows, :].reshape(all_rows, MAIN)
        block = jnp.concatenate([block, block, gg_tail[i]], axis=1)
        for m in range(3):
            w = jnp.dot(block, kw[:, MAIN * m : MAIN * (m + 1)], preferred_element_type=F32)
            wgt[i, m] = w.astype(BF)
        w = jnp.dot(block, kw[:, main:], preferred_element_type=F32)
        for m in range(3):
            wgt_tail[i, m] = moved(w, TAIL * m, TAIL * i).astype(BF)

    def spread_rows(j, factor=None):
        for a in range(moms):
            for k in range(own_k):
                x = gl_r[j, a, own_e * k : own_e * (k + 1), :]
                if factor is not None:
                    x = (x.astype(F32) * factor).astype(BF)
                gl[j, own_k * a + k, :own_e, :] = x
            tails = unpack_tail(gl_r[j, a, rows:, :].astype(F32))
            for k in range(own_k):
                x = jnp.concatenate(tails[3 * k : 3 * (k + 1)], axis=0)
                if factor is not None:
                    x = x * factor
                at = own_k * a + k
                if j < 3:
                    gl_tail[j, at, :own_e, :TAIL] = x[:, :TAIL].astype(BF)
                if j > 0:
                    x = pltpu.roll(x, TAIL, 1)[:, TAIL : 2 * TAIL]
                    gl_tail[j - 1, at, :own_e, TAIL : 2 * TAIL] = x.astype(BF)

    def window(i, step, first=False):
        for m in range(3):
            t = toe[step, m * all_rows : (m + 1) * all_rows, :]
            h = jnp.dot(t, gl[i + step].reshape(span, MAIN), preferred_element_type=F32)
            if first:
                acc[i, m] = h
            else:
                acc[i, m] += h

    def window_tail(step, first=False):
        for m in range(3):
            t = toe[step, m * all_rows : (m + 1) * all_rows, :]
            h = jnp.dot(t, gl_tail[step].reshape(span, 128), preferred_element_type=F32)
            if first:
                acc_tail[m] = h
            else:
                acc_tail[m] += h

    def pair_sums(m, edges, tail_at):
        z = None
        tail = None
        for i, j in edges:
            x = lax.dot_general(
                wgt[i, m], gl[j].reshape(span, MAIN), NT, preferred_element_type=F32
            )
            z = x if z is None else z + x
            tail = wgt_tail[i, m] if tail is None else tail + wgt_tail[i, m]
        z = z + lax.dot_general(
            tail, gl_tail[tail_at].reshape(span, 128), NT, preferred_element_type=F32
        )
        total = None
        for k in range(4):
            a = z[own_e * k : own_e * (k + 1)]
            b = z[own_e * (k + 4) : own_e * (k + 5)]
            lo, hi = turn(a[:, :128] + b[:, 128:], a[:, 128:] + b[:, :128], span - 32 * k)
            total = (lo, hi) if total is None else (total[0] + lo, total[1] + hi)
        return total

    row8 = lax.broadcasted_iota(jnp.int32, (8, 128), 0)

    def diagonals(a, b):
        total = None
        for at in range(0, own_e, 8):
            x = pltpu.roll(a[at : at + 8], (127 - at) % 128, 1)
            x = x + pltpu.roll(b[at : at + 8], (127 + own_e - at) % 128, 1)
            total = x if total is None else total + x
        for bit in (1, 2, 4):
            total = jnp.where(row8 & bit != 0, pltpu.roll(total, 128 - bit, 1), total)
        return total

    await_ring(gl_r, 1, r_gl)
    spread_rows(1)
    spread_rows(2)
    own_sums = [pair_sums(m, ((0, 1), (1, 2)), 1) for m in range(3)]
    up_sums = [pair_sums(m, ((0, 2),), 2) for m in range(3)]
    window(0, 1, True)
    window(1, 1, True)
    window_tail(1, True)
    window(0, 2)
    window(1, 0)
    for a in range(moms):
        landed(gl_r.at[3, a], r_gl.at[3, a])
    spread_rows(3, has_up)
    scale = 1.0 / (NO * np.sqrt(np.float32(momenta * ens * own_e)))
    found = [[], []]
    for m in range(3):
        last = pair_sums(m, ((1, 3),), 2)
        for side in range(2):
            a = jnp.where(spot > row, own_sums[m][side], 0.0)
            b = jnp.where(spot <= row, up_sums[m][side] + last[side], 0.0)
            found[side].append(jnp.sum(diagonals(a, b), axis=0, keepdims=True) * scale)
    part[...] = jnp.concatenate(found[0] + found[1] + [jnp.zeros((2, 128), F32)], axis=0)
    got_z[iz] = part[...]
    for rel in range(1, nz):
        send(remote(part, got_z.at[iz], s_z.at[rel], r_z.at[iz], me, z_of[rel]))

    window(1, 2)
    window_tail(2)
    for a in range(moms):
        landed(gl_r.at[0, a], r_gl.at[0, a])
    spread_rows(0, has_low)
    window(0, 0)
    window_tail(0)
    for i in range(NX):
        tail = sum(moved(acc_tail[m], TAIL * i, TAIL * m) for m in range(3))
        hi, lo = zip(*[split(x) for x in (acc[i, 0], acc[i, 1], acc[i, 2], tail)])
        hi, lo = jnp.concatenate(hi, axis=1), jnp.concatenate(lo, axis=1)
        se = jnp.dot(hi, ks_hi[...], preferred_element_type=F32)
        se = se + jnp.dot(lo, ks_hi[...], preferred_element_type=F32)
        se = se + jnp.dot(hi, ks_lo[...], preferred_element_type=F32)
        tail = jnp.dot(hi, ks_tail[...], preferred_element_type=F32)
        tail = tail + jnp.dot(lo, ks_tail[...], preferred_element_type=F32)
        tail = tail + pltpu.roll(tail, 128 - TAIL, 1)
        se = jnp.concatenate([se, tail], axis=1)
        for a in range(moms):
            x = se[rows * a : rows * (a + 1)]
            se_t[i, a, :rows, :] = x[:, :MAIN].astype(BF)
            se_t[i, a, rows:, :] = pack_tail(x[:, MAIN:]).astype(BF)
    for i, (rx, rm) in enumerate(mates):
        if i:
            send(remote(
                se_t.at[ix_of[rx], mom_of[rm]], se_r.at[pair], s_se.at[i], r_se.at[pair],
                mom_of[rm], ring * NX + ix_of[rx],
            ))
    se_r[pair] = se_t[ix, me]

    for rel in range(1, nz):
        at = lax.rem(iz + rel, nz)
        landed(got_z.at[at], r_z.at[at])
    total = got_z[0]
    for z in range(1, nz):
        total = total + got_z[z]
    for half in range(2):
        plane[half, :3] = total[3 * half : 3 * (half + 1)]
    got_p[iy, pair] = plane[me // (moms // 2)]
    for i, (ry, rx, rm) in enumerate(flats):
        send(remote(
            plane.at[mom_of[rm] // (moms // 2)], got_p.at[iy, pair], s_p.at[i], r_p.at[iy, pair],
            mom_of[rm], (y_of[ry] * nz + iz) * NX + ix_of[rx],
        ))

    for i, (rx, rm) in enumerate(mates):
        if i:
            at = mom_of[rm] * NX + ix_of[rx]
            landed(se_r.at[at], r_se.at[at])
    for p in range(pairs):
        at = pl.ds(p, rows, stride=pairs)
        rows_f.at[0][at, :] = se_r[p, :rows, :128].astype(F32)
        rows_f.at[1][at, :] = se_r[p, :rows, 128:].astype(F32)
        tails = unpack_tail(se_r[p, rows:, :].astype(F32))
        rows_f.at[2][at, :] = jnp.concatenate(tails, axis=0)
    whole = jnp.concatenate([rows_f[0], rows_f[1], rows_f[2, :, :TAIL]], axis=1)
    se_ref[...] = whole.reshape(own_k, own_e, pairs, 2 * NN).astype(BF)

    for ry, rx, rm in flats:
        at = (y_of[ry], mom_of[rm] * NX + ix_of[rx])
        landed(got_p.at[at[0], at[1]], r_p.at[at[0], at[1]])
    own_q = momenta // moms
    for p in range(pairs):
        total = got_p[0, p]
        for y in range(1, ny):
            total = total + got_p[y, p]
        x = jnp.where(lax.rem(me, 2) == 1, pltpu.roll(total, 64, 1), total)
        for q in range(own_q):
            y = pltpu.roll(x, 128 - 32 * q, 1) if q else x
            for m in range(3):
                pol_ref[q, m, p, :] = y[m, :window_n]
    for copy in sent:
        copy.wait_send()


def deliver(se_ref, pol_ref, se_out, pol_out, sems):
    copies = [
        pltpu.make_async_copy(se_ref, se_out, sems.at[0]),
        pltpu.make_async_copy(pol_ref, pol_out, sems.at[1]),
    ]
    for copy in copies:
        copy.start()
    for copy in copies:
        copy.wait()


def body(green_less, green_greater, derivative, neighbours, phonon):
    own_k, own_e, pairs, width = green_less.shape
    momenta, window_n = phonon.shape[1], phonon.shape[2]
    moms, ens = lax.axis_size("mom"), lax.axis_size("en")
    nz = min(8, ens // NX)
    ny = ens // (nz * NX)
    dims = (moms, ens, ny, nz, own_k, own_e, pairs, momenta, window_n)
    mates = moms * NX
    span = 32 * momenta
    rows = own_k * own_e
    all_rows = momenta * own_e
    sent = rows + 8
    constants = [jnp.asarray(t, BF) for t in tables()]
    dma = pltpu.SemaphoreType.DMA
    operands = [
        green_less, green_greater, derivative.transpose(1, 0, 2), neighbours,
        phonon.transpose(0, 1, 3, 4, 2), *constants,
    ]
    order = [0, 1, 2, 4, 5, 6]
    near = [pltpu.VMEM(operands[i].shape, operands[i].dtype) for i in order]
    near.insert(3, pltpu.SMEM(neighbours.shape, neighbours.dtype))
    self_energy, pol = pl.pallas_call(
        functools.partial(kernel, dims),
        out_shape=(
            pltpu.VMEM((own_k, own_e, pairs, width), BF),
            pltpu.VMEM((momenta // moms, 3, pairs, window_n), F32),
        ),
        in_specs=[pl.BlockSpec(memory_space=pl.ANY)] * len(operands),
        out_specs=(pl.BlockSpec(memory_space=pltpu.VMEM),) * 2,
        scratch_shapes=near + [
            pltpu.VMEM((3, rows * pairs, 128), F32),
            pltpu.VMEM((pairs, sent, MAIN), BF),
            pltpu.VMEM((pairs, sent, MAIN), BF),
            pltpu.VMEM((4, moms, sent, MAIN), BF),
            pltpu.VMEM((NX, moms, sent, MAIN), BF),
            pltpu.VMEM((4, momenta, 32, MAIN), BF),
            pltpu.VMEM((3, momenta, 32, 128), BF),
            pltpu.VMEM((NX, all_rows, 128), BF),
            pltpu.VMEM((4, 2, 3 * pairs, 128), F32),
            pltpu.VMEM((3, 3 * all_rows, span), BF),
            pltpu.VMEM((3 * MAIN + 128, MAIN), BF),
            pltpu.VMEM((3 * MAIN + 128, MAIN), BF),
            pltpu.VMEM((3 * MAIN + 128, 128), BF),
            pltpu.VMEM((2 * MAIN + 128, 3 * MAIN + 128), BF),
            pltpu.VMEM((NX, 3, all_rows, MAIN), BF),
            pltpu.VMEM((NX, 3, all_rows, 128), BF),
            pltpu.VMEM((NX, 3, all_rows, MAIN), F32),
            pltpu.VMEM((3, all_rows, 128), F32),
            pltpu.VMEM((NX, moms, sent, MAIN), BF),
            pltpu.VMEM((pairs, sent, MAIN), BF),
            pltpu.VMEM((8, 128), F32),
            pltpu.VMEM((nz, 8, 128), F32),
            pltpu.VMEM((2, 4, 128), F32),
            pltpu.VMEM((ny, pairs, 4, 128), F32),
            dma((len(operands),)), dma((mates,)), dma((NX, moms)), dma((mates,)), dma((mates,)),
            dma((4, moms)), dma((mates,)), dma((pairs,)), dma((nz,)), dma((nz,)),
            dma((ny * mates,)), dma((ny, pairs)),
        ],
        compiler_params=pltpu.CompilerParams(collective_id=0, has_side_effects=True),
    )(*operands)
    self_energy = pltpu.with_memory_space_constraint(self_energy, pltpu.VMEM)
    pol = pltpu.with_memory_space_constraint(pol, pltpu.VMEM)
    self_energy, pol = pl.pallas_call(
        deliver,
        out_shape=tuple(jax.ShapeDtypeStruct(x.shape, x.dtype) for x in (self_energy, pol)),
        in_specs=[pl.BlockSpec(memory_space=pltpu.VMEM)] * 2,
        out_specs=(pl.BlockSpec(memory_space=pl.ANY),) * 2,
        scratch_shapes=[dma((2,))],
        compiler_params=pltpu.CompilerParams(vmem_limit_bytes=16 << 20),
    )(self_energy, pol)
    return self_energy, pol.transpose(0, 3, 1, 2)


def solution(mesh):
    return jax.shard_map(
        body,
        mesh=mesh,
        in_specs=(P("mom", "en", None, None), P("mom", "en", None, None), P(), P(), P()),
        out_specs=(P("mom", "en", None, None), P("mom", None, None, None)),
        check_vma=False,
    )
```

```python
import functools

import jax
import jax.numpy as jnp
import numpy as np
from jax import lax
from jax.experimental import pallas as pl
from jax.experimental.pallas import tpu as pltpu
from jax.sharding import PartitionSpec as P

NO = 12
NB = 4
NN = NO * NO
MAIN = 256
TAIL = 2 * NN - MAIN
WIDE = MAIN + 128
NX = 2
MESH = pl.DeviceIdType.MESH
BF = jnp.bfloat16
F32 = jnp.float32
NT = (((1,), (1,)), ((), ()))


def tables():
    r = np.arange(NN)
    first, second = r // NO, r % NO
    rows = np.zeros((4, NN, NN), np.float32)
    cols = np.zeros((4, NN, WIDE), np.float32)
    sub = np.arange(2 * NN) % NN
    for at, (of_row, own, of_col, other) in enumerate((
        (second, first, first, sub // NO),
        (second, second, first, sub % NO),
        (first, second, second, sub // NO),
        (first, first, second, sub % NO),
    )):
        rows[at] = of_row[None, :] == own[:, None]
        cols[at, :, : 2 * NN] = of_col[:, None] == other[None, :]
    return rows, cols


def split(x):
    hi = x.astype(BF)
    return hi, (x - hi.astype(F32)).astype(BF)


def kernel(
    dims,
    gl_hbm, gg_hbm, der_hbm, nb_hbm, ph_hbm, rt_hbm, ct_hbm,
    se_ref, pol_ref,
    gl_in, gg_in, der_ref, nb_ref, ph_ref, rt_ref, ct_ref,
    rows_f, gl_t, gg_t, gl_r, gg_r, gl, gl_tail, gg_tail, coef, toe, ks_hi, ks_lo, ks_tail, kw,
    wgt, wgt_tail, acc, acc_tail,
    se_t, se_r, part, got_z, plane, got_p,
    loads, s_gg, r_gg, s_own, s_halo, r_gl, s_se, r_se, s_z, r_z, s_p, r_p,
):
    moms, ens, ny, nz, own_k, own_e, pairs, momenta, window_n = dims
    rows = own_k * own_e
    all_rows = momenta * own_e
    span = 32 * momenta
    groups = rows // 8
    me = lax.axis_index("mom")
    en = lax.axis_index("en")
    ring, ix = en // NX, en % NX
    iy, iz = ring // nz, ring % nz
    rings = ens // NX
    above_ring, below_ring = lax.rem(ring + 1, rings), lax.rem(ring + rings - 1, rings)
    pair = me * NX + ix

    hbm = (gl_hbm, gg_hbm, ph_hbm, der_hbm, nb_hbm, rt_hbm, ct_hbm)
    near = (gl_in, gg_in, ph_ref, der_ref, nb_ref, rt_ref, ct_ref)
    fetch = [pltpu.make_async_copy(a, b, loads.at[i]) for i, (a, b) in enumerate(zip(hbm, near))]
    for copy in fetch:
        copy.start()

    barrier = pltpu.get_barrier_semaphore()

    def greet(mom_at, en_at):
        pl.semaphore_signal(
            barrier, inc=1, device_id={"mom": mom_at, "en": en_at}, device_id_type=MESH
        )

    core, far = lax.rem(me, 2), me // 2
    mom_of = [
        (far if rm < 2 else 1 - far) * 2 + (1 - core if rm % 2 else core) for rm in range(moms)
    ]
    ix_of = [ix, 1 - ix]
    mates = [(0, 0)] + [(0, 2), (0, 3), (1, 0), (1, 1), (1, 2), (1, 3), (0, 1)]
    for rx, rm in mates:
        if rx or rm:
            greet(mom_of[rm], ring * NX + ix_of[rx])
    greet(me, above_ring * NX + ix)
    greet(me, below_ring * NX + ix)
    z_of = [(iy * nz + lax.rem(iz + rel, nz)) * NX + ix for rel in range(nz)]
    for rel in range(1, nz):
        greet(me, z_of[rel])
    y_of = [lax.rem(iy + ry, ny) for ry in range(ny)]
    flats = [(ry, rx, rm) for ry in range(ny) for rx in range(NX) for rm in range(moms)][1:]
    for ry, rx, rm in flats:
        if ry:
            greet(mom_of[rm], (y_of[ry] * nz + iz) * NX + ix_of[rx])
    greeted = len(mates) + 1 + nz - 1 + (ny - 1) * len(mates)

    lane8 = lax.broadcasted_iota(jnp.int32, (8, 128), 1)

    def pack_tail(x):
        halves = [jnp.zeros((8, 128), F32), jnp.zeros((8, 128), F32)]
        for g in range(groups):
            y = x[8 * g : 8 * (g + 1)]
            at = TAIL * (g % 4)
            y = pltpu.roll(y, at, 1) if at else y
            keep = (lane8 >= at) & (lane8 < at + TAIL)
            halves[g // 4] = jnp.where(keep, y, halves[g // 4])
        return jnp.concatenate(halves, axis=1)

    def unpack_tail(x):
        found = []
        for g in range(groups):
            y = x[:, 128 * (g // 4) : 128 * (g // 4 + 1)]
            at = TAIL * (g % 4)
            y = pltpu.roll(y, 128 - at, 1) if at else y
            found.append(jnp.where(lane8 < TAIL, y, 0.0))
        return found

    def by_pair(src, dst):
        whole = src[...].astype(F32).reshape(rows * pairs, 2 * NN)
        rows_f[0] = whole[:, :128]
        rows_f[1] = whole[:, 128:MAIN]
        rows_f[2, :, :TAIL] = whole[:, MAIN:]
        for p in range(pairs):
            x = [rows_f.at[c][pl.ds(p, rows, stride=pairs), :] for c in range(3)]
            dst[p, :rows, :128] = x[0].astype(BF)
            dst[p, :rows, 128:] = x[1].astype(BF)
            dst[p, rows:, :] = pack_tail(x[2]).astype(BF)

    def remote(src, dst, send, recv, mom_at, en_at):
        return pltpu.make_async_remote_copy(
            src_ref=src, dst_ref=dst, send_sem=send, recv_sem=recv,
            device_id={"mom": mom_at, "en": en_at}, device_id_type=MESH,
        )

    def landed(ref, sem):
        pltpu.make_async_copy(ref, ref, sem).wait()

    sent = []

    def send(copy):
        copy.start()
        sent.append(copy)

    def to_ring(source, buffer, first, sends, recvs):
        for i, (rx, rm) in enumerate(mates):
            if i:
                to = mom_of[rm] * NX + ix_of[rx]
                send(remote(
                    source.at[to], buffer.at[first + ix, me], sends.at[i], recvs.at[first + ix, me],
                    mom_of[rm], ring * NX + ix_of[rx],
                ))

    fetch[0].wait()
    by_pair(gl_in, gl_t)
    pl.semaphore_wait(barrier, greeted)
    to_ring(gl_t, gl_r, 1, s_own, r_gl)
    gl_r[1 + ix, me] = gl_t[pair]
    fetch[1].wait()
    by_pair(gg_in, gg_t)
    to_ring(gg_t, gg_r, 0, s_gg, r_gg)
    gg_r[ix, me] = gg_t[pair]

    def await_ring(buffer, first, sems):
        for i, (rx, rm) in enumerate(mates):
            if i:
                at = first + ix_of[rx]
                landed(buffer.at[at, mom_of[rm]], sems.at[at, mom_of[rm]])

    gl[:, :, own_e:, :] = jnp.zeros((4, momenta, 32 - own_e, MAIN), BF)
    gl_tail[...] = jnp.zeros((3, momenta, 32, 128), BF)

    for copy in fetch[2:]:
        copy.wait()

    first_part = lax.broadcasted_iota(jnp.int32, (NN, WIDE), 1) < NN
    pair_lane = lax.broadcasted_iota(jnp.int32, (NN, 128), 1)

    def expand(row, rows_of, cols_of):
        hi, lo = split(row)
        out = jnp.dot(rows_of * hi, cols_of, preferred_element_type=F32)
        return out + jnp.dot(rows_of * lo, cols_of, preferred_element_type=F32)

    def block_of(m, index):
        found = der_ref[m, 0:1, :]
        for i in range(1, der_ref.shape[1]):
            found = jnp.where(index == i, der_ref[m, i : i + 1, :], found)
        return found

    cut = MAIN - NN
    other = nb_ref[pair // NB, lax.rem(pair, NB)]
    main = 3 * MAIN
    ks_hi[main + 3 * TAIL :, :] = jnp.zeros((128 - 3 * TAIL, MAIN), BF)
    ks_lo[main + 3 * TAIL :, :] = jnp.zeros((128 - 3 * TAIL, MAIN), BF)
    ks_tail[...] = jnp.zeros((main + 128, 128), BF)
    kw[2 * MAIN :, :] = jnp.zeros((128, main + 128), BF)
    kw[:, main + 96 :] = jnp.zeros((2 * MAIN + 128, 32), BF)
    for m in range(3):
        left, right = block_of(m, pair // NB), block_of(m, other)
        both = expand(left, rt_ref[0], ct_ref[0]) * expand(right, rt_ref[1], ct_ref[1])
        tops = split(jnp.where(first_part, both, 0.0))
        lows = split(jnp.where(first_part, 0.0, both))
        at = MAIN * m
        tail_at = main + TAIL * m
        for dst, top, low in zip((ks_hi, ks_lo), tops, lows):
            dst[at : at + NN, :] = top[:, :MAIN]
            dst[at + NN : at + MAIN, :] = low[:cut, :MAIN]
            dst[tail_at : tail_at + TAIL, :] = low[cut:, :MAIN]
        last = jnp.where(first_part, 0.0, both)[:, MAIN:]
        hi = last.astype(BF).astype(F32)
        last = jnp.where(pair_lane < TAIL, hi, pltpu.roll(last - hi, TAIL, 1)).astype(BF)
        ks_tail[at + NN : at + MAIN, :] = last[:cut]
        ks_tail[tail_at : tail_at + TAIL, :] = last[cut:]
        both = expand(left, rt_ref[2], ct_ref[2]) * expand(right, rt_ref[3], ct_ref[3])
        top = jnp.where(first_part, both, 0.0)
        low = jnp.where(first_part, 0.0, -both)
        shift = lambda x: pltpu.roll(x[:, MAIN:], TAIL * m, 1) if m else x[:, MAIN:]
        lane_at = slice(main + TAIL * m, main + TAIL * (m + 1))
        last = split(shift(low))
        for half, (x, y, z) in enumerate(zip(split(top), split(low), last)):
            z = z[:, TAIL * m : TAIL * (m + 1)]
            row_at, rest = MAIN * half, 2 * MAIN + TAIL * half
            kw[row_at : row_at + NN, at : at + MAIN] = x[:, :MAIN]
            kw[row_at + NN : row_at + MAIN, at : at + MAIN] = y[:cut, :MAIN]
            kw[rest : rest + TAIL, at : at + MAIN] = y[cut:, :MAIN]
            kw[row_at : row_at + NN, lane_at] = jnp.zeros((NN, TAIL), BF)
            kw[row_at + NN : row_at + MAIN, lane_at] = z[:cut]
            kw[rest : rest + TAIL, lane_at] = z[cut:]

    lane = lax.broadcasted_iota(jnp.int32, (own_e, 128), 1)
    row = lax.broadcasted_iota(jnp.int32, (own_e, 128), 0)
    spot = lax.rem(lane, 32)

    def turn(lo, hi, n):
        n = n % span
        if n >= 128:
            lo, hi, n = hi, lo, n - 128
        if n == 0:
            return lo, hi
        a, b = pltpu.roll(lo, n, 1), pltpu.roll(hi, n, 1)
        keep = lane >= n
        return jnp.where(keep, a, b), jnp.where(keep, b, a)

    def slide(at, index):
        lo, hi = (coef.at[at, side][pl.ds(index, own_e, stride=0), :] for side in range(2))
        a = pltpu.roll(lo, 0, 1, stride=1, stride_axis=0)
        b = pltpu.roll(hi, 0, 1, stride=1, stride_axis=0)
        keep = lane >= row
        return jnp.where(keep, a, b), jnp.where(keep, b, a)

    lines = 3 * pairs
    w_at = lax.broadcasted_iota(jnp.int32, (window_n, 128), 0)
    l_at = lax.broadcasted_iota(jnp.int32, (window_n, 128), 1)
    places = (l_at == window_n - 1 - w_at, l_at == w_at)
    for s in range(2):
        flat = ph_ref[s].reshape(momenta * lines, window_n)
        spread = jnp.dot(
            flat, jnp.where(places[s], 1.0, 0.0).astype(BF), preferred_element_type=F32
        )
        sides = [None, None]
        for q in range(momenta):
            block = (momenta - q) % momenta
            x = spread[lines * q : lines * (q + 1)]
            if block % 4:
                x = pltpu.roll(x, 32 * (block % 4), 1)
            sides[block // 4] = x if sides[block // 4] is None else sides[block // 4] + x
        for at, n in ((2 * s, (0, 1)[s]), (2 * s + 1, (span - window_n, span + 1 - window_n)[s])):
            lo, hi = turn(sides[0], sides[1], n)
            coef[at, 0] = lo
            coef[at, 1] = hi

    for m in range(3):
        index = m * pairs + pair
        absorb, absorb_own = slide(0, index), slide(1, index)
        emit_own, emit = slide(2, index), slide(3, index)
        for step in range(3):
            pick = []
            for side in range(2):
                if step == 0:
                    x = jnp.where(spot >= row, absorb[side], 0.0)
                elif step == 1:
                    x = jnp.where(spot >= row, emit_own[side], absorb_own[side])
                else:
                    x = jnp.where(spot <= row, emit[side], 0.0)
                pick.append(x)
            for k in range(0, momenta, 2):
                even, odd = turn(*pick, 32 * k), turn(*pick, 32 * (k + 1))
                at = m * all_rows + k * own_e
                for side in range(2):
                    both = jnp.concatenate([even[side], odd[side]], axis=0)
                    toe[step, at : at + 2 * own_e, 128 * side : 128 * (side + 1)] = both.astype(BF)

    for i, (rx, rm) in enumerate(mates):
        half, a = ix_of[rx], mom_of[rm]
        if i:
            landed(gl_r.at[1 + half, a], r_gl.at[1 + half, a])
            source = gl_r.at[1 + half, a]
        else:
            source = gl_t.at[pair]
        target = lax.rem(ring + rings + 2 * half - 1, rings)
        slot = 3 - 3 * half
        send(remote(
            source, gl_r.at[slot, a], s_halo.at[i], r_gl.at[slot, a], me, target * NX + ix,
        ))

    has_low = (ring > 0).astype(F32)
    has_up = (ring < rings - 1).astype(F32)
    tail_lane = lax.broadcasted_iota(jnp.int32, (all_rows, 128), 1)

    def moved(x, source, target):
        n = (target - source) % 128
        x = pltpu.roll(x, n, 1) if n else x
        return jnp.where((tail_lane >= target) & (tail_lane < target + TAIL), x, 0.0)

    await_ring(gg_r, 0, r_gg)
    for i in range(NX):
        for a in range(moms):
            tails = unpack_tail(gg_r[i, a, rows:, :].astype(F32))
            tails = [x + pltpu.roll(x, TAIL, 1) for x in tails]
            gg_tail[i, rows * a : rows * (a + 1), :] = jnp.concatenate(tails, axis=0).astype(BF)
        block = gg_r[i, :, :rows, :].reshape(all_rows, MAIN)
        block = jnp.concatenate([block, block, gg_tail[i]], axis=1)
        for m in range(3):
            w = jnp.dot(block, kw[:, MAIN * m : MAIN * (m + 1)], preferred_element_type=F32)
            wgt[i, m] = w.astype(BF)
        w = jnp.dot(block, kw[:, main:], preferred_element_type=F32)
        for m in range(3):
            wgt_tail[i, m] = moved(w, TAIL * m, TAIL * i).astype(BF)

    def spread_rows(j, factor=None):
        for a in range(moms):
            for k in range(own_k):
                x = gl_r[j, a, own_e * k : own_e * (k + 1), :]
                if factor is not None:
                    x = (x.astype(F32) * factor).astype(BF)
                gl[j, own_k * a + k, :own_e, :] = x
            tails = unpack_tail(gl_r[j, a, rows:, :].astype(F32))
            for k in range(own_k):
                x = jnp.concatenate(tails[3 * k : 3 * (k + 1)], axis=0)
                if factor is not None:
                    x = x * factor
                at = own_k * a + k
                if j < 3:
                    gl_tail[j, at, :own_e, :TAIL] = x[:, :TAIL].astype(BF)
                if j > 0:
                    x = pltpu.roll(x, TAIL, 1)[:, TAIL : 2 * TAIL]
                    gl_tail[j - 1, at, :own_e, TAIL : 2 * TAIL] = x.astype(BF)

    def window(i, step, first=False):
        for m in range(3):
            t = toe[step, m * all_rows : (m + 1) * all_rows, :]
            h = jnp.dot(t, gl[i + step].reshape(span, MAIN), preferred_element_type=F32)
            if first:
                acc[i, m] = h
            else:
                acc[i, m] += h

    def window_tail(step, first=False):
        for m in range(3):
            t = toe[step, m * all_rows : (m + 1) * all_rows, :]
            h = jnp.dot(t, gl_tail[step].reshape(span, 128), preferred_element_type=F32)
            if first:
                acc_tail[m] = h
            else:
                acc_tail[m] += h

    def pair_sums(m, edges, tail_at):
        z = None
        tail = None
        for i, j in edges:
            x = lax.dot_general(
                wgt[i, m], gl[j].reshape(span, MAIN), NT, preferred_element_type=F32
            )
            z = x if z is None else z + x
            tail = wgt_tail[i, m] if tail is None else tail + wgt_tail[i, m]
        z = z + lax.dot_general(
            tail, gl_tail[tail_at].reshape(span, 128), NT, preferred_element_type=F32
        )
        total = None
        for k in range(4):
            a = z[own_e * k : own_e * (k + 1)]
            b = z[own_e * (k + 4) : own_e * (k + 5)]
            lo, hi = turn(a[:, :128] + b[:, 128:], a[:, 128:] + b[:, :128], span - 32 * k)
            total = (lo, hi) if total is None else (total[0] + lo, total[1] + hi)
        return total

    row8 = lax.broadcasted_iota(jnp.int32, (8, 128), 0)

    def diagonals(a, b):
        total = None
        for at in range(0, own_e, 8):
            x = pltpu.roll(a[at : at + 8], (127 - at) % 128, 1)
            x = x + pltpu.roll(b[at : at + 8], (127 + own_e - at) % 128, 1)
            total = x if total is None else total + x
        for bit in (1, 2, 4):
            total = jnp.where(row8 & bit != 0, pltpu.roll(total, 128 - bit, 1), total)
        return total

    spread_rows(1)
    spread_rows(2)
    own_sums = [pair_sums(m, ((0, 1), (1, 2)), 1) for m in range(3)]
    up_sums = [pair_sums(m, ((0, 2),), 2) for m in range(3)]
    window(0, 1, True)
    window(1, 1, True)
    window_tail(1, True)
    window(0, 2)
    window(1, 0)
    for a in range(moms):
        landed(gl_r.at[3, a], r_gl.at[3, a])
    spread_rows(3, has_up)
    scale = 1.0 / (NO * np.sqrt(np.float32(momenta * ens * own_e)))
    found = [[], []]
    for m in range(3):
        last = pair_sums(m, ((1, 3),), 2)
        for side in range(2):
            a = jnp.where(spot > row, own_sums[m][side], 0.0)
            b = jnp.where(spot <= row, up_sums[m][side] + last[side], 0.0)
            found[side].append(jnp.sum(diagonals(a, b), axis=0, keepdims=True) * scale)
    part[...] = jnp.concatenate(found[0] + found[1] + [jnp.zeros((2, 128), F32)], axis=0)
    got_z[iz] = part[...]
    for rel in range(1, nz):
        send(remote(part, got_z.at[iz], s_z.at[rel], r_z.at[iz], me, z_of[rel]))

    window(1, 2)
    window_tail(2)
    for a in range(moms):
        landed(gl_r.at[0, a], r_gl.at[0, a])
    spread_rows(0, has_low)
    window(0, 0)
    window_tail(0)
    for i in range(NX):
        tail = sum(moved(acc_tail[m], TAIL * i, TAIL * m) for m in range(3))
        hi, lo = zip(*[split(x) for x in (acc[i, 0], acc[i, 1], acc[i, 2], tail)])
        hi, lo = jnp.concatenate(hi, axis=1), jnp.concatenate(lo, axis=1)
        se = jnp.dot(hi, ks_hi[...], preferred_element_type=F32)
        se = se + jnp.dot(lo, ks_hi[...], preferred_element_type=F32)
        se = se + jnp.dot(hi, ks_lo[...], preferred_element_type=F32)
        tail = jnp.dot(hi, ks_tail[...], preferred_element_type=F32)
        tail = tail + jnp.dot(lo, ks_tail[...], preferred_element_type=F32)
        tail = tail + pltpu.roll(tail, 128 - TAIL, 1)
        se = jnp.concatenate([se, tail], axis=1)
        for a in range(moms):
            x = se[rows * a : rows * (a + 1)]
            se_t[i, a, :rows, :] = x[:, :MAIN].astype(BF)
            se_t[i, a, rows:, :] = pack_tail(x[:, MAIN:]).astype(BF)
    for i, (rx, rm) in enumerate(mates):
        if i:
            send(remote(
                se_t.at[ix_of[rx], mom_of[rm]], se_r.at[pair], s_se.at[i], r_se.at[pair],
                mom_of[rm], ring * NX + ix_of[rx],
            ))
    se_r[pair] = se_t[ix, me]

    for rel in range(1, nz):
        at = lax.rem(iz + rel, nz)
        landed(got_z.at[at], r_z.at[at])
    total = got_z[0]
    for z in range(1, nz):
        total = total + got_z[z]
    for half in range(2):
        plane[half, :3] = total[3 * half : 3 * (half + 1)]
    got_p[iy, pair] = plane[me // (moms // 2)]
    for i, (ry, rx, rm) in enumerate(flats):
        send(remote(
            plane.at[mom_of[rm] // (moms // 2)], got_p.at[iy, pair], s_p.at[i], r_p.at[iy, pair],
            mom_of[rm], (y_of[ry] * nz + iz) * NX + ix_of[rx],
        ))

    for i, (rx, rm) in enumerate(mates):
        if i:
            at = mom_of[rm] * NX + ix_of[rx]
            landed(se_r.at[at], r_se.at[at])
    for p in range(pairs):
        at = pl.ds(p, rows, stride=pairs)
        rows_f.at[0][at, :] = se_r[p, :rows, :128].astype(F32)
        rows_f.at[1][at, :] = se_r[p, :rows, 128:].astype(F32)
        tails = unpack_tail(se_r[p, rows:, :].astype(F32))
        rows_f.at[2][at, :] = jnp.concatenate(tails, axis=0)
    whole = jnp.concatenate([rows_f[0], rows_f[1], rows_f[2, :, :TAIL]], axis=1)
    se_ref[...] = whole.reshape(own_k, own_e, pairs, 2 * NN).astype(BF)

    for ry, rx, rm in flats:
        at = (y_of[ry], mom_of[rm] * NX + ix_of[rx])
        landed(got_p.at[at[0], at[1]], r_p.at[at[0], at[1]])
    own_q = momenta // moms
    for p in range(pairs):
        total = got_p[0, p]
        for y in range(1, ny):
            total = total + got_p[y, p]
        x = jnp.where(lax.rem(me, 2) == 1, pltpu.roll(total, 64, 1), total)
        for q in range(own_q):
            y = pltpu.roll(x, 128 - 32 * q, 1) if q else x
            for m in range(3):
                pol_ref[q, m, p, :] = y[m, :window_n]
    for copy in sent:
        copy.wait_send()


def deliver(se_ref, pol_ref, se_out, pol_out, sems):
    copies = [
        pltpu.make_async_copy(se_ref, se_out, sems.at[0]),
        pltpu.make_async_copy(pol_ref, pol_out, sems.at[1]),
    ]
    for copy in copies:
        copy.start()
    for copy in copies:
        copy.wait()


def body(green_less, green_greater, derivative, neighbours, phonon):
    own_k, own_e, pairs, width = green_less.shape
    momenta, window_n = phonon.shape[1], phonon.shape[2]
    moms, ens = lax.axis_size("mom"), lax.axis_size("en")
    nz = min(8, ens // NX)
    ny = ens // (nz * NX)
    dims = (moms, ens, ny, nz, own_k, own_e, pairs, momenta, window_n)
    mates = moms * NX
    span = 32 * momenta
    rows = own_k * own_e
    all_rows = momenta * own_e
    sent = rows + 8
    constants = [jnp.asarray(t, BF) for t in tables()]
    dma = pltpu.SemaphoreType.DMA
    operands = [
        green_less, green_greater, derivative.transpose(1, 0, 2), neighbours,
        phonon.transpose(0, 1, 3, 4, 2), *constants,
    ]
    order = [0, 1, 2, 4, 5, 6]
    near = [pltpu.VMEM(operands[i].shape, operands[i].dtype) for i in order]
    near.insert(3, pltpu.SMEM(neighbours.shape, neighbours.dtype))
    self_energy, pol = pl.pallas_call(
        functools.partial(kernel, dims),
        out_shape=(
            pltpu.VMEM((own_k, own_e, pairs, width), BF),
            pltpu.VMEM((momenta // moms, 3, pairs, window_n), F32),
        ),
        in_specs=[pl.BlockSpec(memory_space=pl.ANY)] * len(operands),
        out_specs=(pl.BlockSpec(memory_space=pltpu.VMEM),) * 2,
        scratch_shapes=near + [
            pltpu.VMEM((3, rows * pairs, 128), F32),
            pltpu.VMEM((pairs, sent, MAIN), BF),
            pltpu.VMEM((pairs, sent, MAIN), BF),
            pltpu.VMEM((4, moms, sent, MAIN), BF),
            pltpu.VMEM((NX, moms, sent, MAIN), BF),
            pltpu.VMEM((4, momenta, 32, MAIN), BF),
            pltpu.VMEM((3, momenta, 32, 128), BF),
            pltpu.VMEM((NX, all_rows, 128), BF),
            pltpu.VMEM((4, 2, 3 * pairs, 128), F32),
            pltpu.VMEM((3, 3 * all_rows, span), BF),
            pltpu.VMEM((3 * MAIN + 128, MAIN), BF),
            pltpu.VMEM((3 * MAIN + 128, MAIN), BF),
            pltpu.VMEM((3 * MAIN + 128, 128), BF),
            pltpu.VMEM((2 * MAIN + 128, 3 * MAIN + 128), BF),
            pltpu.VMEM((NX, 3, all_rows, MAIN), BF),
            pltpu.VMEM((NX, 3, all_rows, 128), BF),
            pltpu.VMEM((NX, 3, all_rows, MAIN), F32),
            pltpu.VMEM((3, all_rows, 128), F32),
            pltpu.VMEM((NX, moms, sent, MAIN), BF),
            pltpu.VMEM((pairs, sent, MAIN), BF),
            pltpu.VMEM((8, 128), F32),
            pltpu.VMEM((nz, 8, 128), F32),
            pltpu.VMEM((2, 4, 128), F32),
            pltpu.VMEM((ny, pairs, 4, 128), F32),
            dma((len(operands),)), dma((mates,)), dma((NX, moms)), dma((mates,)), dma((mates,)),
            dma((4, moms)), dma((mates,)), dma((pairs,)), dma((nz,)), dma((nz,)),
            dma((ny * mates,)), dma((ny, pairs)),
        ],
        compiler_params=pltpu.CompilerParams(collective_id=0, has_side_effects=True),
    )(*operands)
    self_energy = pltpu.with_memory_space_constraint(self_energy, pltpu.VMEM)
    pol = pltpu.with_memory_space_constraint(pol, pltpu.VMEM)
    self_energy, pol = pl.pallas_call(
        deliver,
        out_shape=tuple(jax.ShapeDtypeStruct(x.shape, x.dtype) for x in (self_energy, pol)),
        in_specs=[pl.BlockSpec(memory_space=pltpu.VMEM)] * 2,
        out_specs=(pl.BlockSpec(memory_space=pl.ANY),) * 2,
        scratch_shapes=[dma((2,))],
        compiler_params=pltpu.CompilerParams(vmem_limit_bytes=16 << 20),
    )(self_energy, pol)
    return self_energy, pol.transpose(0, 3, 1, 2)


def solution(mesh):
    return jax.shard_map(
        body,
        mesh=mesh,
        in_specs=(P("mom", "en", None, None), P("mom", "en", None, None), P(), P(), P()),
        out_specs=(P("mom", "en", None, None), P("mom", None, None, None)),
        check_vma=False,
    )
```

```python
import functools

import jax
import jax.numpy as jnp
import numpy as np
from jax import lax
from jax.experimental import pallas as pl
from jax.experimental.pallas import tpu as pltpu
from jax.sharding import PartitionSpec as P

NO = 12
NB = 4
NN = NO * NO
MAIN = 256
TAIL = 2 * NN - MAIN
WIDE = MAIN + 128
NX = 2
MESH = pl.DeviceIdType.MESH
BF = jnp.bfloat16
F32 = jnp.float32
NT = (((1,), (1,)), ((), ()))


def tables():
    r = np.arange(NN)
    first, second = r // NO, r % NO
    rows = np.zeros((4, NN, NN), np.float32)
    cols = np.zeros((4, NN, WIDE), np.float32)
    sub = np.arange(2 * NN) % NN
    for at, (of_row, own, of_col, other) in enumerate((
        (second, first, first, sub // NO),
        (second, second, first, sub % NO),
        (first, second, second, sub // NO),
        (first, first, second, sub % NO),
    )):
        rows[at] = of_row[None, :] == own[:, None]
        cols[at, :, : 2 * NN] = of_col[:, None] == other[None, :]
    return rows, cols


def split(x):
    hi = x.astype(BF)
    return hi, (x - hi.astype(F32)).astype(BF)


def kernel(
    dims,
    gl_hbm, gg_hbm, der_hbm, nb_hbm, ph_hbm, rt_hbm, ct_hbm,
    se_ref, pol_ref,
    gl_in, gg_in, der_ref, nb_ref, ph_ref, rt_ref, ct_ref,
    rows_f, gl_t, gg_t, gl_r, gg_r, gl, gl_tail, gg_tail, coef, toe, ks_hi, ks_lo, ks_tail, kw,
    wgt, wgt_tail, acc, acc_tail,
    se_t, se_r, part, got_z, plane, got_p,
    loads, s_gg, r_gg, s_own, s_halo, r_gl, s_se, r_se, s_z, r_z, s_p, r_p, first_word, second_word,
):
    moms, ens, ny, nz, own_k, own_e, pairs, momenta, window_n = dims
    rows = own_k * own_e
    all_rows = momenta * own_e
    span = 32 * momenta
    groups = rows // 8
    me = lax.axis_index("mom")
    en = lax.axis_index("en")
    ring, ix = en // NX, en % NX
    iy, iz = ring // nz, ring % nz
    rings = ens // NX
    above_ring, below_ring = lax.rem(ring + 1, rings), lax.rem(ring + rings - 1, rings)
    pair = me * NX + ix

    hbm = (gl_hbm, gg_hbm, ph_hbm, der_hbm, nb_hbm, rt_hbm, ct_hbm)
    near = (gl_in, gg_in, ph_ref, der_ref, nb_ref, rt_ref, ct_ref)
    fetch = [pltpu.make_async_copy(a, b, loads.at[i]) for i, (a, b) in enumerate(zip(hbm, near))]
    for copy in fetch:
        copy.start()

    barrier = pltpu.get_barrier_semaphore()

    def greet(mom_at, en_at):
        pl.semaphore_signal(
            barrier, inc=1, device_id={"mom": mom_at, "en": en_at}, device_id_type=MESH
        )

    core, far = lax.rem(me, 2), me // 2
    mom_of = [
        (far if rm < 2 else 1 - far) * 2 + (1 - core if rm % 2 else core) for rm in range(moms)
    ]
    ix_of = [ix, 1 - ix]
    mates = [(0, 0)] + [(0, 2), (1, 0), (0, 3), (1, 1), (1, 2), (1, 3), (0, 1)]
    for rx, rm in mates:
        if rx or rm:
            greet(mom_of[rm], ring * NX + ix_of[rx])
    greet(me, above_ring * NX + ix)
    greet(me, below_ring * NX + ix)
    z_of = [(iy * nz + lax.rem(iz + rel, nz)) * NX + ix for rel in range(nz)]
    y_of = [lax.rem(iy + ry, ny) for ry in range(ny)]
    line_of = [(y_of[ry] * nz + iz) * NX + ix for ry in range(ny)]
    flats = [(ry, rx, rm) for ry in range(ny) for rx in range(NX) for rm in range(moms)][1:]
    next_to = [z_of[1], z_of[nz - 1], line_of[1], line_of[ny - 1]]
    beyond = [z_of[2], z_of[nz - 2], line_of[2]]
    for to in next_to:
        greet(me, to)
    greeted = len(mates) + 1 + len(next_to)

    def tell(word, devices):
        for to in devices:
            pl.semaphore_signal(
                word, inc=1, device_id={"mom": me, "en": to}, device_id_type=MESH
            )

    lane8 = lax.broadcasted_iota(jnp.int32, (8, 128), 1)

    def pack_tail(x):
        halves = [jnp.zeros((8, 128), F32), jnp.zeros((8, 128), F32)]
        for g in range(groups):
            y = x[8 * g : 8 * (g + 1)]
            at = TAIL * (g % 4)
            y = pltpu.roll(y, at, 1) if at else y
            keep = (lane8 >= at) & (lane8 < at + TAIL)
            halves[g // 4] = jnp.where(keep, y, halves[g // 4])
        return jnp.concatenate(halves, axis=1)

    def unpack_tail(x):
        found = []
        for g in range(groups):
            y = x[:, 128 * (g // 4) : 128 * (g // 4 + 1)]
            at = TAIL * (g % 4)
            y = pltpu.roll(y, 128 - at, 1) if at else y
            found.append(jnp.where(lane8 < TAIL, y, 0.0))
        return found

    def by_pair(src, dst):
        whole = src[...].astype(F32).reshape(rows * pairs, 2 * NN)
        rows_f[0] = whole[:, :128]
        rows_f[1] = whole[:, 128:MAIN]
        rows_f[2, :, :TAIL] = whole[:, MAIN:]
        for p in range(pairs):
            x = [rows_f.at[c][pl.ds(p, rows, stride=pairs), :] for c in range(3)]
            dst[p, :rows, :128] = x[0].astype(BF)
            dst[p, :rows, 128:] = x[1].astype(BF)
            dst[p, rows:, :] = pack_tail(x[2]).astype(BF)

    def remote(src, dst, send, recv, mom_at, en_at):
        return pltpu.make_async_remote_copy(
            src_ref=src, dst_ref=dst, send_sem=send, recv_sem=recv,
            device_id={"mom": mom_at, "en": en_at}, device_id_type=MESH,
        )

    def landed(ref, sem):
        pltpu.make_async_copy(ref, ref, sem).wait()

    sent = []

    def send(copy):
        copy.start()
        sent.append(copy)

    def to_ring(source, buffer, first, sends, recvs):
        for i, (rx, rm) in enumerate(mates):
            if i:
                to = mom_of[rm] * NX + ix_of[rx]
                send(remote(
                    source.at[to], buffer.at[first + ix, me], sends.at[i], recvs.at[first + ix, me],
                    mom_of[rm], ring * NX + ix_of[rx],
                ))

    fetch[0].wait()
    by_pair(gl_in, gl_t)
    pl.semaphore_wait(barrier, greeted)
    tell(first_word, next_to)
    to_ring(gl_t, gl_r, 1, s_own, r_gl)
    gl_r[1 + ix, me] = gl_t[pair]
    fetch[1].wait()
    by_pair(gg_in, gg_t)
    to_ring(gg_t, gg_r, 0, s_gg, r_gg)
    gg_r[ix, me] = gg_t[pair]

    def await_ring(buffer, first, sems):
        for i, (rx, rm) in enumerate(mates):
            if i:
                at = first + ix_of[rx]
                landed(buffer.at[at, mom_of[rm]], sems.at[at, mom_of[rm]])

    gl[:, :, own_e:, :] = jnp.zeros((4, momenta, 32 - own_e, MAIN), BF)
    gl_tail[...] = jnp.zeros((3, momenta, 32, 128), BF)

    for copy in fetch[2:]:
        copy.wait()

    first_part = lax.broadcasted_iota(jnp.int32, (NN, WIDE), 1) < NN
    pair_lane = lax.broadcasted_iota(jnp.int32, (NN, 128), 1)

    def expand(row, rows_of, cols_of):
        hi, lo = split(row)
        out = jnp.dot(rows_of * hi, cols_of, preferred_element_type=F32)
        return out + jnp.dot(rows_of * lo, cols_of, preferred_element_type=F32)

    def block_of(m, index):
        found = der_ref[m, 0:1, :]
        for i in range(1, der_ref.shape[1]):
            found = jnp.where(index == i, der_ref[m, i : i + 1, :], found)
        return found

    cut = MAIN - NN
    other = nb_ref[pair // NB, lax.rem(pair, NB)]
    main = 3 * MAIN
    ks_hi[main + 3 * TAIL :, :] = jnp.zeros((128 - 3 * TAIL, MAIN), BF)
    ks_lo[main + 3 * TAIL :, :] = jnp.zeros((128 - 3 * TAIL, MAIN), BF)
    ks_tail[...] = jnp.zeros((main + 128, 128), BF)
    kw[2 * MAIN :, :] = jnp.zeros((128, main + 128), BF)
    kw[:, main + 96 :] = jnp.zeros((2 * MAIN + 128, 32), BF)
    for m in range(3):
        left, right = block_of(m, pair // NB), block_of(m, other)
        both = expand(left, rt_ref[0], ct_ref[0]) * expand(right, rt_ref[1], ct_ref[1])
        tops = split(jnp.where(first_part, both, 0.0))
        lows = split(jnp.where(first_part, 0.0, both))
        at = MAIN * m
        tail_at = main + TAIL * m
        for dst, top, low in zip((ks_hi, ks_lo), tops, lows):
            dst[at : at + NN, :] = top[:, :MAIN]
            dst[at + NN : at + MAIN, :] = low[:cut, :MAIN]
            dst[tail_at : tail_at + TAIL, :] = low[cut:, :MAIN]
        last = jnp.where(first_part, 0.0, both)[:, MAIN:]
        hi = last.astype(BF).astype(F32)
        last = jnp.where(pair_lane < TAIL, hi, pltpu.roll(last - hi, TAIL, 1)).astype(BF)
        ks_tail[at + NN : at + MAIN, :] = last[:cut]
        ks_tail[tail_at : tail_at + TAIL, :] = last[cut:]
        both = expand(left, rt_ref[2], ct_ref[2]) * expand(right, rt_ref[3], ct_ref[3])
        top = jnp.where(first_part, both, 0.0)
        low = jnp.where(first_part, 0.0, -both)
        shift = lambda x: pltpu.roll(x[:, MAIN:], TAIL * m, 1) if m else x[:, MAIN:]
        lane_at = slice(main + TAIL * m, main + TAIL * (m + 1))
        last = split(shift(low))
        for half, (x, y, z) in enumerate(zip(split(top), split(low), last)):
            z = z[:, TAIL * m : TAIL * (m + 1)]
            row_at, rest = MAIN * half, 2 * MAIN + TAIL * half
            kw[row_at : row_at + NN, at : at + MAIN] = x[:, :MAIN]
            kw[row_at + NN : row_at + MAIN, at : at + MAIN] = y[:cut, :MAIN]
            kw[rest : rest + TAIL, at : at + MAIN] = y[cut:, :MAIN]
            kw[row_at : row_at + NN, lane_at] = jnp.zeros((NN, TAIL), BF)
            kw[row_at + NN : row_at + MAIN, lane_at] = z[:cut]
            kw[rest : rest + TAIL, lane_at] = z[cut:]

    pl.semaphore_wait(first_word, len(next_to))
    tell(second_word, beyond)

    lane = lax.broadcasted_iota(jnp.int32, (own_e, 128), 1)
    row = lax.broadcasted_iota(jnp.int32, (own_e, 128), 0)
    spot = lax.rem(lane, 32)

    def turn(lo, hi, n):
        n = n % span
        if n >= 128:
            lo, hi, n = hi, lo, n - 128
        if n == 0:
            return lo, hi
        a, b = pltpu.roll(lo, n, 1), pltpu.roll(hi, n, 1)
        keep = lane >= n
        return jnp.where(keep, a, b), jnp.where(keep, b, a)

    def slide(at, index):
        lo, hi = (coef.at[at, side][pl.ds(index, own_e, stride=0), :] for side in range(2))
        a = pltpu.roll(lo, 0, 1, stride=1, stride_axis=0)
        b = pltpu.roll(hi, 0, 1, stride=1, stride_axis=0)
        keep = lane >= row
        return jnp.where(keep, a, b), jnp.where(keep, b, a)

    lines = 3 * pairs
    w_at = lax.broadcasted_iota(jnp.int32, (window_n, 128), 0)
    l_at = lax.broadcasted_iota(jnp.int32, (window_n, 128), 1)
    places = (l_at == window_n - 1 - w_at, l_at == w_at)
    for s in range(2):
        flat = ph_ref[s].reshape(momenta * lines, window_n)
        spread = jnp.dot(
            flat, jnp.where(places[s], 1.0, 0.0).astype(BF), preferred_element_type=F32
        )
        sides = [None, None]
        for q in range(momenta):
            block = (momenta - q) % momenta
            x = spread[lines * q : lines * (q + 1)]
            if block % 4:
                x = pltpu.roll(x, 32 * (block % 4), 1)
            sides[block // 4] = x if sides[block // 4] is None else sides[block // 4] + x
        for at, n in ((2 * s, (0, 1)[s]), (2 * s + 1, (span - window_n, span + 1 - window_n)[s])):
            lo, hi = turn(sides[0], sides[1], n)
            coef[at, 0] = lo
            coef[at, 1] = hi

    for m in range(3):
        index = m * pairs + pair
        absorb, absorb_own = slide(0, index), slide(1, index)
        emit_own, emit = slide(2, index), slide(3, index)
        for step in range(3):
            pick = []
            for side in range(2):
                if step == 0:
                    x = jnp.where(spot >= row, absorb[side], 0.0)
                elif step == 1:
                    x = jnp.where(spot >= row, emit_own[side], absorb_own[side])
                else:
                    x = jnp.where(spot <= row, emit[side], 0.0)
                pick.append(x)
            for k in range(0, momenta, 2):
                even, odd = turn(*pick, 32 * k), turn(*pick, 32 * (k + 1))
                at = m * all_rows + k * own_e
                for side in range(2):
                    both = jnp.concatenate([even[side], odd[side]], axis=0)
                    toe[step, at : at + 2 * own_e, 128 * side : 128 * (side + 1)] = both.astype(BF)

    for half in range(NX):
        target, slot = ((below_ring, 3), (above_ring, 0))[half]
        for rm in (0, 1, 2, 3):
            a = mom_of[rm]
            if rm:
                landed(gl_r.at[1 + half, a], r_gl.at[1 + half, a])
            else:
                @pl.when(ix != half)
                def _():
                    landed(gl_r.at[1 + half, a], r_gl.at[1 + half, a])
            send(remote(
                gl_r.at[1 + half, a], gl_r.at[slot, a], s_halo.at[moms * half + rm],
                r_gl.at[slot, a], me, target * NX + ix,
            ))

    pl.semaphore_wait(second_word, len(beyond))

    has_low = (ring > 0).astype(F32)
    has_up = (ring < rings - 1).astype(F32)
    tail_lane = lax.broadcasted_iota(jnp.int32, (all_rows, 128), 1)

    def moved(x, source, target):
        n = (target - source) % 128
        x = pltpu.roll(x, n, 1) if n else x
        return jnp.where((tail_lane >= target) & (tail_lane < target + TAIL), x, 0.0)

    await_ring(gg_r, 0, r_gg)
    for i in range(NX):
        for a in range(moms):
            tails = unpack_tail(gg_r[i, a, rows:, :].astype(F32))
            tails = [x + pltpu.roll(x, TAIL, 1) for x in tails]
            gg_tail[i, rows * a : rows * (a + 1), :] = jnp.concatenate(tails, axis=0).astype(BF)
        block = gg_r[i, :, :rows, :].reshape(all_rows, MAIN)
        block = jnp.concatenate([block, block, gg_tail[i]], axis=1)
        for m in range(3):
            w = jnp.dot(block, kw[:, MAIN * m : MAIN * (m + 1)], preferred_element_type=F32)
            wgt[i, m] = w.astype(BF)
        w = jnp.dot(block, kw[:, main:], preferred_element_type=F32)
        for m in range(3):
            wgt_tail[i, m] = moved(w, TAIL * m, TAIL * i).astype(BF)

    def spread_rows(j, factor=None):
        for a in range(moms):
            for k in range(own_k):
                x = gl_r[j, a, own_e * k : own_e * (k + 1), :]
                if factor is not None:
                    x = (x.astype(F32) * factor).astype(BF)
                gl[j, own_k * a + k, :own_e, :] = x
            tails = unpack_tail(gl_r[j, a, rows:, :].astype(F32))
            for k in range(own_k):
                x = jnp.concatenate(tails[3 * k : 3 * (k + 1)], axis=0)
                if factor is not None:
                    x = x * factor
                at = own_k * a + k
                if j < 3:
                    gl_tail[j, at, :own_e, :TAIL] = x[:, :TAIL].astype(BF)
                if j > 0:
                    x = pltpu.roll(x, TAIL, 1)[:, TAIL : 2 * TAIL]
                    gl_tail[j - 1, at, :own_e, TAIL : 2 * TAIL] = x.astype(BF)

    def window(i, step, first=False):
        for m in range(3):
            t = toe[step, m * all_rows : (m + 1) * all_rows, :]
            h = jnp.dot(t, gl[i + step].reshape(span, MAIN), preferred_element_type=F32)
            if first:
                acc[i, m] = h
            else:
                acc[i, m] += h

    def window_tail(step, first=False):
        for m in range(3):
            t = toe[step, m * all_rows : (m + 1) * all_rows, :]
            h = jnp.dot(t, gl_tail[step].reshape(span, 128), preferred_element_type=F32)
            if first:
                acc_tail[m] = h
            else:
                acc_tail[m] += h

    def pair_sums(m, edges, tail_at):
        z = None
        tail = None
        for i, j in edges:
            x = lax.dot_general(
                wgt[i, m], gl[j].reshape(span, MAIN), NT, preferred_element_type=F32
            )
            z = x if z is None else z + x
            tail = wgt_tail[i, m] if tail is None else tail + wgt_tail[i, m]
        z = z + lax.dot_general(
            tail, gl_tail[tail_at].reshape(span, 128), NT, preferred_element_type=F32
        )
        total = None
        for k in range(4):
            a = z[own_e * k : own_e * (k + 1)]
            b = z[own_e * (k + 4) : own_e * (k + 5)]
            lo, hi = turn(a[:, :128] + b[:, 128:], a[:, 128:] + b[:, :128], span - 32 * k)
            total = (lo, hi) if total is None else (total[0] + lo, total[1] + hi)
        return total

    row8 = lax.broadcasted_iota(jnp.int32, (8, 128), 0)

    def diagonals(a, b):
        total = None
        for at in range(0, own_e, 8):
            x = pltpu.roll(a[at : at + 8], (127 - at) % 128, 1)
            x = x + pltpu.roll(b[at : at + 8], (127 + own_e - at) % 128, 1)
            total = x if total is None else total + x
        for bit in (1, 2, 4):
            total = jnp.where(row8 & bit != 0, pltpu.roll(total, 128 - bit, 1), total)
        return total

    spread_rows(1)
    spread_rows(2)
    own_sums = [pair_sums(m, ((0, 1), (1, 2)), 1) for m in range(3)]
    up_sums = [pair_sums(m, ((0, 2),), 2) for m in range(3)]
    window(0, 1, True)
    window(1, 1, True)
    window_tail(1, True)
    window(0, 2)
    window(1, 0)
    for a in range(moms):
        landed(gl_r.at[3, a], r_gl.at[3, a])
    spread_rows(3, has_up)
    scale = 1.0 / (NO * np.sqrt(np.float32(momenta * ens * own_e)))
    found = [[], []]
    for m in range(3):
        last = pair_sums(m, ((1, 3),), 2)
        for side in range(2):
            a = jnp.where(spot > row, own_sums[m][side], 0.0)
            b = jnp.where(spot <= row, up_sums[m][side] + last[side], 0.0)
            found[side].append(jnp.sum(diagonals(a, b), axis=0, keepdims=True) * scale)
    part[...] = jnp.concatenate(found[0] + found[1] + [jnp.zeros((2, 128), F32)], axis=0)
    got_z[iz] = part[...]
    for rel in range(1, nz):
        send(remote(part, got_z.at[iz], s_z.at[rel], r_z.at[iz], me, z_of[rel]))

    window(1, 2)
    window_tail(2)
    for a in range(moms):
        landed(gl_r.at[0, a], r_gl.at[0, a])
    spread_rows(0, has_low)
    window(0, 0)
    window_tail(0)
    for i in range(NX):
        tail = sum(moved(acc_tail[m], TAIL * i, TAIL * m) for m in range(3))
        hi, lo = zip(*[split(x) for x in (acc[i, 0], acc[i, 1], acc[i, 2], tail)])
        hi, lo = jnp.concatenate(hi, axis=1), jnp.concatenate(lo, axis=1)
        se = jnp.dot(hi, ks_hi[...], preferred_element_type=F32)
        se = se + jnp.dot(lo, ks_hi[...], preferred_element_type=F32)
        se = se + jnp.dot(hi, ks_lo[...], preferred_element_type=F32)
        tail = jnp.dot(hi, ks_tail[...], preferred_element_type=F32)
        tail = tail + jnp.dot(lo, ks_tail[...], preferred_element_type=F32)
        tail = tail + pltpu.roll(tail, 128 - TAIL, 1)
        se = jnp.concatenate([se, tail], axis=1)
        for a in range(moms):
            x = se[rows * a : rows * (a + 1)]
            se_t[i, a, :rows, :] = x[:, :MAIN].astype(BF)
            se_t[i, a, rows:, :] = pack_tail(x[:, MAIN:]).astype(BF)
    for i, (rx, rm) in enumerate(mates):
        if i:
            send(remote(
                se_t.at[ix_of[rx], mom_of[rm]], se_r.at[pair], s_se.at[i], r_se.at[pair],
                mom_of[rm], ring * NX + ix_of[rx],
            ))
    se_r[pair] = se_t[ix, me]

    for rel in range(1, nz):
        at = lax.rem(iz + rel, nz)
        landed(got_z.at[at], r_z.at[at])
    total = got_z[0]
    for z in range(1, nz):
        total = total + got_z[z]
    swung = pltpu.roll(total, 64, 1)
    for a in range(moms):
        at = 3 * (a // 2)
        low, high = (total, swung) if a % 2 == 0 else (swung, total)
        plane[a, 0:1] = jnp.where(lane8[:1] < 64, low[at : at + 1], high[at + 1 : at + 2])
        plane[a, 1:2] = low[at + 2 : at + 3]
    got_p[iy, pair] = plane[me]
    for i, (ry, rx, rm) in enumerate(flats):
        send(remote(
            plane.at[mom_of[rm]], got_p.at[iy, pair], s_p.at[i], r_p.at[iy, pair],
            mom_of[rm], (y_of[ry] * nz + iz) * NX + ix_of[rx],
        ))

    for i, (rx, rm) in enumerate(mates):
        if i:
            at = mom_of[rm] * NX + ix_of[rx]
            landed(se_r.at[at], r_se.at[at])
    for p in range(pairs):
        at = pl.ds(p, rows, stride=pairs)
        rows_f.at[0][at, :] = se_r[p, :rows, :128].astype(F32)
        rows_f.at[1][at, :] = se_r[p, :rows, 128:].astype(F32)
        tails = unpack_tail(se_r[p, rows:, :].astype(F32))
        rows_f.at[2][at, :] = jnp.concatenate(tails, axis=0)
    whole = jnp.concatenate([rows_f[0], rows_f[1], rows_f[2, :, :TAIL]], axis=1)
    se_ref[...] = whole.reshape(own_k, own_e, pairs, 2 * NN).astype(BF)

    for ry, rx, rm in flats:
        at = (y_of[ry], mom_of[rm] * NX + ix_of[rx])
        landed(got_p.at[at[0], at[1]], r_p.at[at[0], at[1]])
    own_q = momenta // moms
    for p in range(pairs):
        total = got_p[0, p]
        for y in range(1, ny):
            total = total + got_p[y, p]
        for q in range(own_q):
            for m in range(3):
                at = 64 * (m % 2) + 32 * q
                y = pltpu.roll(total, 128 - at, 1) if at else total
                pol_ref[q, m, p, :] = y[m // 2, :window_n]
    for copy in sent:
        copy.wait_send()


def deliver(se_ref, pol_ref, se_out, pol_out, sems):
    copies = [
        pltpu.make_async_copy(se_ref, se_out, sems.at[0]),
        pltpu.make_async_copy(pol_ref, pol_out, sems.at[1]),
    ]
    for copy in copies:
        copy.start()
    for copy in copies:
        copy.wait()


def body(green_less, green_greater, derivative, neighbours, phonon):
    own_k, own_e, pairs, width = green_less.shape
    momenta, window_n = phonon.shape[1], phonon.shape[2]
    moms, ens = lax.axis_size("mom"), lax.axis_size("en")
    nz = min(8, ens // NX)
    ny = ens // (nz * NX)
    dims = (moms, ens, ny, nz, own_k, own_e, pairs, momenta, window_n)
    mates = moms * NX
    span = 32 * momenta
    rows = own_k * own_e
    all_rows = momenta * own_e
    sent = rows + 8
    constants = [jnp.asarray(t, BF) for t in tables()]
    dma = pltpu.SemaphoreType.DMA
    operands = [
        green_less, green_greater, derivative.transpose(1, 0, 2), neighbours,
        phonon.transpose(0, 1, 3, 4, 2), *constants,
    ]
    order = [0, 1, 2, 4, 5, 6]
    near = [pltpu.VMEM(operands[i].shape, operands[i].dtype) for i in order]
    near.insert(3, pltpu.SMEM(neighbours.shape, neighbours.dtype))
    self_energy, pol = pl.pallas_call(
        functools.partial(kernel, dims),
        out_shape=(
            pltpu.VMEM((own_k, own_e, pairs, width), BF),
            pltpu.VMEM((momenta // moms, 3, pairs, window_n), F32),
        ),
        in_specs=[pl.BlockSpec(memory_space=pl.ANY)] * len(operands),
        out_specs=(pl.BlockSpec(memory_space=pltpu.VMEM),) * 2,
        scratch_shapes=near + [
            pltpu.VMEM((3, rows * pairs, 128), F32),
            pltpu.VMEM((pairs, sent, MAIN), BF),
            pltpu.VMEM((pairs, sent, MAIN), BF),
            pltpu.VMEM((4, moms, sent, MAIN), BF),
            pltpu.VMEM((NX, moms, sent, MAIN), BF),
            pltpu.VMEM((4, momenta, 32, MAIN), BF),
            pltpu.VMEM((3, momenta, 32, 128), BF),
            pltpu.VMEM((NX, all_rows, 128), BF),
            pltpu.VMEM((4, 2, 3 * pairs, 128), F32),
            pltpu.VMEM((3, 3 * all_rows, span), BF),
            pltpu.VMEM((3 * MAIN + 128, MAIN), BF),
            pltpu.VMEM((3 * MAIN + 128, MAIN), BF),
            pltpu.VMEM((3 * MAIN + 128, 128), BF),
            pltpu.VMEM((2 * MAIN + 128, 3 * MAIN + 128), BF),
            pltpu.VMEM((NX, 3, all_rows, MAIN), BF),
            pltpu.VMEM((NX, 3, all_rows, 128), BF),
            pltpu.VMEM((NX, 3, all_rows, MAIN), F32),
            pltpu.VMEM((3, all_rows, 128), F32),
            pltpu.VMEM((NX, moms, sent, MAIN), BF),
            pltpu.VMEM((pairs, sent, MAIN), BF),
            pltpu.VMEM((8, 128), F32),
            pltpu.VMEM((nz, 8, 128), F32),
            pltpu.VMEM((moms, 2, 128), F32),
            pltpu.VMEM((ny, pairs, 2, 128), F32),
            dma((len(operands),)), dma((mates,)), dma((NX, moms)), dma((mates,)), dma((mates,)),
            dma((4, moms)), dma((mates,)), dma((pairs,)), dma((nz,)), dma((nz,)),
            dma((ny * mates,)), dma((ny, pairs)),
            pltpu.SemaphoreType.REGULAR, pltpu.SemaphoreType.REGULAR,
        ],
        compiler_params=pltpu.CompilerParams(collective_id=0, has_side_effects=True),
    )(*operands)
    self_energy = pltpu.with_memory_space_constraint(self_energy, pltpu.VMEM)
    pol = pltpu.with_memory_space_constraint(pol, pltpu.VMEM)
    self_energy, pol = pl.pallas_call(
        deliver,
        out_shape=tuple(jax.ShapeDtypeStruct(x.shape, x.dtype) for x in (self_energy, pol)),
        in_specs=[pl.BlockSpec(memory_space=pltpu.VMEM)] * 2,
        out_specs=(pl.BlockSpec(memory_space=pl.ANY),) * 2,
        scratch_shapes=[dma((2,))],
        compiler_params=pltpu.CompilerParams(vmem_limit_bytes=16 << 20),
    )(self_energy, pol)
    return self_energy, pol.transpose(0, 3, 1, 2)


def solution(mesh):
    return jax.shard_map(
        body,
        mesh=mesh,
        in_specs=(P("mom", "en", None, None), P("mom", "en", None, None), P(), P(), P()),
        out_specs=(P("mom", "en", None, None), P("mom", None, None, None)),
        check_vma=False,
    )
```

```python
import functools

import jax
import jax.numpy as jnp
import numpy as np
from jax import lax
from jax.experimental import pallas as pl
from jax.experimental.pallas import tpu as pltpu
from jax.sharding import PartitionSpec as P

NO = 12
NB = 4
NN = NO * NO
MAIN = 256
TAIL = 2 * NN - MAIN
WIDE = MAIN + 128
NX = 2
MESH = pl.DeviceIdType.MESH
BF = jnp.bfloat16
F32 = jnp.float32
NT = (((1,), (1,)), ((), ()))


def tables():
    r = np.arange(NN)
    first, second = r // NO, r % NO
    rows = np.zeros((4, NN, NN), np.float32)
    cols = np.zeros((4, NN, WIDE), np.float32)
    sub = np.arange(2 * NN) % NN
    for at, (of_row, own, of_col, other) in enumerate((
        (second, first, first, sub // NO),
        (second, second, first, sub % NO),
        (first, second, second, sub // NO),
        (first, first, second, sub % NO),
    )):
        rows[at] = of_row[None, :] == own[:, None]
        cols[at, :, : 2 * NN] = of_col[:, None] == other[None, :]
    return rows, cols


def split(x):
    hi = x.astype(BF)
    return hi, (x - hi.astype(F32)).astype(BF)


def kernel(
    dims,
    gl_hbm, gg_hbm, der_hbm, nb_hbm, ph_hbm, rt_hbm, ct_hbm,
    se_ref, pol_ref,
    gl_in, gg_in, der_ref, nb_ref, ph_ref, rt_ref, ct_ref,
    rows_f, gl_t, gg_t, gl_r, gg_r, gl, gl_tail, gg_tail, coef, toe, ks_hi, ks_lo, ks_tail, kw,
    wgt, wgt_tail, acc, acc_tail,
    se_t, se_r, part, got_z, plane, got_p,
    loads, s_gg, r_gg, s_own, s_halo, r_gl, s_se, r_se, s_z, r_z, s_p, r_p, first_word, second_word,
):
    moms, ens, ny, nz, own_k, own_e, pairs, momenta, window_n = dims
    rows = own_k * own_e
    all_rows = momenta * own_e
    span = 32 * momenta
    groups = rows // 8
    me = lax.axis_index("mom")
    en = lax.axis_index("en")
    ring, ix = en // NX, en % NX
    iy, iz = ring // nz, ring % nz
    rings = ens // NX
    above_ring, below_ring = lax.rem(ring + 1, rings), lax.rem(ring + rings - 1, rings)
    pair = me * NX + ix

    hbm = (gl_hbm, gg_hbm, ph_hbm, der_hbm, nb_hbm, rt_hbm, ct_hbm)
    near = (gl_in, gg_in, ph_ref, der_ref, nb_ref, rt_ref, ct_ref)
    fetch = [pltpu.make_async_copy(a, b, loads.at[i]) for i, (a, b) in enumerate(zip(hbm, near))]
    for copy in fetch:
        copy.start()

    barrier = pltpu.get_barrier_semaphore()

    def greet(mom_at, en_at):
        pl.semaphore_signal(
            barrier, inc=1, device_id={"mom": mom_at, "en": en_at}, device_id_type=MESH
        )

    core, far = lax.rem(me, 2), me // 2
    mom_of = [
        (far if rm < 2 else 1 - far) * 2 + (1 - core if rm % 2 else core) for rm in range(moms)
    ]
    ix_of = [ix, 1 - ix]
    mates = [(0, 0)] + [(0, 2), (1, 0), (0, 3), (1, 1), (1, 2), (1, 3), (0, 1)]
    for rx, rm in mates:
        if rx or rm:
            greet(mom_of[rm], ring * NX + ix_of[rx])
    greet(me, above_ring * NX + ix)
    greet(me, below_ring * NX + ix)
    z_of = [(iy * nz + lax.rem(iz + rel, nz)) * NX + ix for rel in range(nz)]
    y_of = [lax.rem(iy + ry, ny) for ry in range(ny)]
    line_of = [(y_of[ry] * nz + iz) * NX + ix for ry in range(ny)]
    flats = [(ry, rx, rm) for ry in range(ny) for rx in range(NX) for rm in range(moms)][1:]
    next_to = [z_of[1], z_of[nz - 1], line_of[1], line_of[ny - 1]]
    beyond = [z_of[2], z_of[nz - 2], line_of[2]]
    for to in next_to:
        greet(me, to)
    greeted = len(mates) + 1 + len(next_to)

    def tell(word, devices):
        for to in devices:
            pl.semaphore_signal(
                word, inc=1, device_id={"mom": me, "en": to}, device_id_type=MESH
            )

    lane8 = lax.broadcasted_iota(jnp.int32, (8, 128), 1)

    def pack_tail(x):
        halves = [jnp.zeros((8, 128), F32), jnp.zeros((8, 128), F32)]
        for g in range(groups):
            y = x[8 * g : 8 * (g + 1)]
            at = TAIL * (g % 4)
            y = pltpu.roll(y, at, 1) if at else y
            keep = (lane8 >= at) & (lane8 < at + TAIL)
            halves[g // 4] = jnp.where(keep, y, halves[g // 4])
        return jnp.concatenate(halves, axis=1)

    def unpack_tail(x):
        found = []
        for g in range(groups):
            y = x[:, 128 * (g // 4) : 128 * (g // 4 + 1)]
            at = TAIL * (g % 4)
            y = pltpu.roll(y, 128 - at, 1) if at else y
            found.append(jnp.where(lane8 < TAIL, y, 0.0))
        return found

    def by_pair(src, dst):
        whole = src[...].astype(F32).reshape(rows * pairs, 2 * NN)
        rows_f[0] = whole[:, :128]
        rows_f[1] = whole[:, 128:MAIN]
        rows_f[2, :, :TAIL] = whole[:, MAIN:]
        for p in range(pairs):
            x = [rows_f.at[c][pl.ds(p, rows, stride=pairs), :] for c in range(3)]
            dst[p, :rows, :128] = x[0].astype(BF)
            dst[p, :rows, 128:] = x[1].astype(BF)
            dst[p, rows:, :] = pack_tail(x[2]).astype(BF)

    def remote(src, dst, send, recv, mom_at, en_at):
        return pltpu.make_async_remote_copy(
            src_ref=src, dst_ref=dst, send_sem=send, recv_sem=recv,
            device_id={"mom": mom_at, "en": en_at}, device_id_type=MESH,
        )

    def landed(ref, sem):
        pltpu.make_async_copy(ref, ref, sem).wait()

    sent = []

    def send(copy):
        copy.start()
        sent.append(copy)

    def to_ring(source, buffer, first, sends, recvs):
        for i, (rx, rm) in enumerate(mates):
            if i:
                to = mom_of[rm] * NX + ix_of[rx]
                send(remote(
                    source.at[to], buffer.at[first + ix, me], sends.at[i], recvs.at[first + ix, me],
                    mom_of[rm], ring * NX + ix_of[rx],
                ))

    fetch[0].wait()
    by_pair(gl_in, gl_t)
    pl.semaphore_wait(barrier, greeted)
    tell(first_word, next_to)
    to_ring(gl_t, gl_r, 1, s_own, r_gl)
    gl_r[1 + ix, me] = gl_t[pair]
    fetch[1].wait()
    by_pair(gg_in, gg_t)
    to_ring(gg_t, gg_r, 0, s_gg, r_gg)
    gg_r[ix, me] = gg_t[pair]

    def await_ring(buffer, first, sems):
        for i, (rx, rm) in enumerate(mates):
            if i:
                at = first + ix_of[rx]
                landed(buffer.at[at, mom_of[rm]], sems.at[at, mom_of[rm]])

    gl[:, :, own_e:, :] = jnp.zeros((4, momenta, 32 - own_e, MAIN), BF)
    gl_tail[...] = jnp.zeros((3, momenta, 32, 128), BF)

    for copy in fetch[2:]:
        copy.wait()

    first_part = lax.broadcasted_iota(jnp.int32, (NN, WIDE), 1) < NN
    pair_lane = lax.broadcasted_iota(jnp.int32, (NN, 128), 1)

    def expand(row, rows_of, cols_of):
        hi, lo = split(row)
        out = jnp.dot(rows_of * hi, cols_of, preferred_element_type=F32)
        return out + jnp.dot(rows_of * lo, cols_of, preferred_element_type=F32)

    def block_of(m, index):
        found = der_ref[m, 0:1, :]
        for i in range(1, der_ref.shape[1]):
            found = jnp.where(index == i, der_ref[m, i : i + 1, :], found)
        return found

    cut = MAIN - NN
    other = nb_ref[pair // NB, lax.rem(pair, NB)]
    main = 3 * MAIN
    ks_hi[main + 3 * TAIL :, :] = jnp.zeros((128 - 3 * TAIL, MAIN), BF)
    ks_lo[main + 3 * TAIL :, :] = jnp.zeros((128 - 3 * TAIL, MAIN), BF)
    ks_tail[...] = jnp.zeros((main + 128, 128), BF)
    kw[2 * MAIN :, :] = jnp.zeros((128, main + 128), BF)
    kw[:, main + 96 :] = jnp.zeros((2 * MAIN + 128, 32), BF)
    for m in range(3):
        left, right = block_of(m, pair // NB), block_of(m, other)
        both = expand(left, rt_ref[0], ct_ref[0]) * expand(right, rt_ref[1], ct_ref[1])
        tops = split(jnp.where(first_part, both, 0.0))
        lows = split(jnp.where(first_part, 0.0, both))
        at = MAIN * m
        tail_at = main + TAIL * m
        for dst, top, low in zip((ks_hi, ks_lo), tops, lows):
            dst[at : at + NN, :] = top[:, :MAIN]
            dst[at + NN : at + MAIN, :] = low[:cut, :MAIN]
            dst[tail_at : tail_at + TAIL, :] = low[cut:, :MAIN]
        last = jnp.where(first_part, 0.0, both)[:, MAIN:]
        hi = last.astype(BF).astype(F32)
        last = jnp.where(pair_lane < TAIL, hi, pltpu.roll(last - hi, TAIL, 1)).astype(BF)
        ks_tail[at + NN : at + MAIN, :] = last[:cut]
        ks_tail[tail_at : tail_at + TAIL, :] = last[cut:]
        both = expand(left, rt_ref[2], ct_ref[2]) * expand(right, rt_ref[3], ct_ref[3])
        top = jnp.where(first_part, both, 0.0)
        low = jnp.where(first_part, 0.0, -both)
        shift = lambda x: pltpu.roll(x[:, MAIN:], TAIL * m, 1) if m else x[:, MAIN:]
        lane_at = slice(main + TAIL * m, main + TAIL * (m + 1))
        last = split(shift(low))
        for half, (x, y, z) in enumerate(zip(split(top), split(low), last)):
            z = z[:, TAIL * m : TAIL * (m + 1)]
            row_at, rest = MAIN * half, 2 * MAIN + TAIL * half
            kw[row_at : row_at + NN, at : at + MAIN] = x[:, :MAIN]
            kw[row_at + NN : row_at + MAIN, at : at + MAIN] = y[:cut, :MAIN]
            kw[rest : rest + TAIL, at : at + MAIN] = y[cut:, :MAIN]
            kw[row_at : row_at + NN, lane_at] = jnp.zeros((NN, TAIL), BF)
            kw[row_at + NN : row_at + MAIN, lane_at] = z[:cut]
            kw[rest : rest + TAIL, lane_at] = z[cut:]

    pl.semaphore_wait(first_word, len(next_to))
    tell(second_word, beyond)

    lane = lax.broadcasted_iota(jnp.int32, (own_e, 128), 1)
    row = lax.broadcasted_iota(jnp.int32, (own_e, 128), 0)
    spot = lax.rem(lane, 32)

    def turn(lo, hi, n):
        n = n % span
        if n >= 128:
            lo, hi, n = hi, lo, n - 128
        if n == 0:
            return lo, hi
        a, b = pltpu.roll(lo, n, 1), pltpu.roll(hi, n, 1)
        keep = lane >= n
        return jnp.where(keep, a, b), jnp.where(keep, b, a)

    def slide(at, index):
        lo, hi = (coef.at[at, side][pl.ds(index, own_e, stride=0), :] for side in range(2))
        a = pltpu.roll(lo, 0, 1, stride=1, stride_axis=0)
        b = pltpu.roll(hi, 0, 1, stride=1, stride_axis=0)
        keep = lane >= row
        return jnp.where(keep, a, b), jnp.where(keep, b, a)

    lines = 3 * pairs
    w_at = lax.broadcasted_iota(jnp.int32, (window_n, 128), 0)
    l_at = lax.broadcasted_iota(jnp.int32, (window_n, 128), 1)
    places = (l_at == window_n - 1 - w_at, l_at == w_at)
    for s in range(2):
        flat = ph_ref[s].reshape(momenta * lines, window_n)
        spread = jnp.dot(
            flat, jnp.where(places[s], 1.0, 0.0).astype(BF), preferred_element_type=F32
        )
        sides = [None, None]
        for q in range(momenta):
            block = (momenta - q) % momenta
            x = spread[lines * q : lines * (q + 1)]
            if block % 4:
                x = pltpu.roll(x, 32 * (block % 4), 1)
            sides[block // 4] = x if sides[block // 4] is None else sides[block // 4] + x
        for at, n in ((2 * s, (0, 1)[s]), (2 * s + 1, (span - window_n, span + 1 - window_n)[s])):
            lo, hi = turn(sides[0], sides[1], n)
            coef[at, 0] = lo
            coef[at, 1] = hi

    for m in range(3):
        index = m * pairs + pair
        absorb, absorb_own = slide(0, index), slide(1, index)
        emit_own, emit = slide(2, index), slide(3, index)
        for step in range(3):
            pick = []
            for side in range(2):
                if step == 0:
                    x = jnp.where(spot >= row, absorb[side], 0.0)
                elif step == 1:
                    x = jnp.where(spot >= row, emit_own[side], absorb_own[side])
                else:
                    x = jnp.where(spot <= row, emit[side], 0.0)
                pick.append(x)
            for k in range(0, momenta, 2):
                even, odd = turn(*pick, 32 * k), turn(*pick, 32 * (k + 1))
                at = m * all_rows + k * own_e
                for side in range(2):
                    both = jnp.concatenate([even[side], odd[side]], axis=0)
                    toe[step, at : at + 2 * own_e, 128 * side : 128 * (side + 1)] = both.astype(BF)

    for half in range(NX):
        target, slot = ((below_ring, 3), (above_ring, 0))[half]
        for rm in (0, 1, 2, 3):
            a = mom_of[rm]
            if rm:
                landed(gl_r.at[1 + half, a], r_gl.at[1 + half, a])
            else:
                @pl.when(ix != half)
                def _():
                    landed(gl_r.at[1 + half, a], r_gl.at[1 + half, a])
            send(remote(
                gl_r.at[1 + half, a], gl_r.at[slot, a], s_halo.at[moms * half + rm],
                r_gl.at[slot, a], me, target * NX + ix,
            ))

    pl.semaphore_wait(second_word, len(beyond))

    has_low = (ring > 0).astype(F32)
    has_up = (ring < rings - 1).astype(F32)
    tail_lane = lax.broadcasted_iota(jnp.int32, (all_rows, 128), 1)

    def moved(x, source, target):
        n = (target - source) % 128
        x = pltpu.roll(x, n, 1) if n else x
        return jnp.where((tail_lane >= target) & (tail_lane < target + TAIL), x, 0.0)

    await_ring(gg_r, 0, r_gg)
    for i in range(NX):
        for a in range(moms):
            tails = unpack_tail(gg_r[i, a, rows:, :].astype(F32))
            tails = [x + pltpu.roll(x, TAIL, 1) for x in tails]
            gg_tail[i, rows * a : rows * (a + 1), :] = jnp.concatenate(tails, axis=0).astype(BF)
        block = gg_r[i, :, :rows, :].reshape(all_rows, MAIN)
        block = jnp.concatenate([block, block, gg_tail[i]], axis=1)
        for m in range(3):
            w = jnp.dot(block, kw[:, MAIN * m : MAIN * (m + 1)], preferred_element_type=F32)
            wgt[i, m] = w.astype(BF)
        w = jnp.dot(block, kw[:, main:], preferred_element_type=F32)
        for m in range(3):
            wgt_tail[i, m] = moved(w, TAIL * m, TAIL * i).astype(BF)

    def spread_rows(j, factor=None):
        for a in range(moms):
            for k in range(own_k):
                x = gl_r[j, a, own_e * k : own_e * (k + 1), :]
                if factor is not None:
                    x = (x.astype(F32) * factor).astype(BF)
                gl[j, own_k * a + k, :own_e, :] = x
            tails = unpack_tail(gl_r[j, a, rows:, :].astype(F32))
            for k in range(own_k):
                x = jnp.concatenate(tails[3 * k : 3 * (k + 1)], axis=0)
                if factor is not None:
                    x = x * factor
                at = own_k * a + k
                if j < 3:
                    gl_tail[j, at, :own_e, :TAIL] = x[:, :TAIL].astype(BF)
                if j > 0:
                    x = pltpu.roll(x, TAIL, 1)[:, TAIL : 2 * TAIL]
                    gl_tail[j - 1, at, :own_e, TAIL : 2 * TAIL] = x.astype(BF)

    def window(i, step, first=False):
        for m in range(3):
            t = toe[step, m * all_rows : (m + 1) * all_rows, :]
            h = jnp.dot(t, gl[i + step].reshape(span, MAIN), preferred_element_type=F32)
            if first:
                acc[i, m] = h
            else:
                acc[i, m] += h

    def window_tail(step, first=False):
        for m in range(3):
            t = toe[step, m * all_rows : (m + 1) * all_rows, :]
            h = jnp.dot(t, gl_tail[step].reshape(span, 128), preferred_element_type=F32)
            if first:
                acc_tail[m] = h
            else:
                acc_tail[m] += h

    def pair_sums(m, edges, tail_at):
        z = None
        tail = None
        for i, j in edges:
            x = lax.dot_general(
                wgt[i, m], gl[j].reshape(span, MAIN), NT, preferred_element_type=F32
            )
            z = x if z is None else z + x
            tail = wgt_tail[i, m] if tail is None else tail + wgt_tail[i, m]
        z = z + lax.dot_general(
            tail, gl_tail[tail_at].reshape(span, 128), NT, preferred_element_type=F32
        )
        total = None
        for k in range(4):
            a = z[own_e * k : own_e * (k + 1)]
            b = z[own_e * (k + 4) : own_e * (k + 5)]
            lo, hi = turn(a[:, :128] + b[:, 128:], a[:, 128:] + b[:, :128], span - 32 * k)
            total = (lo, hi) if total is None else (total[0] + lo, total[1] + hi)
        return total

    row8 = lax.broadcasted_iota(jnp.int32, (8, 128), 0)

    def diagonals(a, b):
        total = None
        for at in range(0, own_e, 8):
            x = pltpu.roll(a[at : at + 8], (127 - at) % 128, 1)
            x = x + pltpu.roll(b[at : at + 8], (127 + own_e - at) % 128, 1)
            total = x if total is None else total + x
        for bit in (1, 2, 4):
            total = jnp.where(row8 & bit != 0, pltpu.roll(total, 128 - bit, 1), total)
        return total

    spread_rows(1)
    spread_rows(2)
    own_sums = [pair_sums(m, ((0, 1), (1, 2)), 1) for m in range(3)]
    up_sums = [pair_sums(m, ((0, 2),), 2) for m in range(3)]
    window(0, 1, True)
    window(1, 1, True)
    window_tail(1, True)
    window(0, 2)
    window(1, 0)
    for a in range(moms):
        landed(gl_r.at[3, a], r_gl.at[3, a])
    spread_rows(3, has_up)
    scale = 1.0 / (NO * np.sqrt(np.float32(momenta * ens * own_e)))
    found = [[], []]
    for m in range(3):
        last = pair_sums(m, ((1, 3),), 2)
        for side in range(2):
            a = jnp.where(spot > row, own_sums[m][side], 0.0)
            b = jnp.where(spot <= row, up_sums[m][side] + last[side], 0.0)
            found[side].append(jnp.sum(diagonals(a, b), axis=0, keepdims=True) * scale)
    part[...] = jnp.concatenate(found[0] + found[1] + [jnp.zeros((2, 128), F32)], axis=0)
    got_z[iz] = part[...]
    for rel in range(1, nz):
        send(remote(part, got_z.at[iz], s_z.at[rel], r_z.at[iz], me, z_of[rel]))

    window(1, 2)
    window_tail(2)
    for rel in range(1, nz):
        at = lax.rem(iz + rel, nz)
        landed(got_z.at[at], r_z.at[at])
    total = got_z[0]
    for z in range(1, nz):
        total = total + got_z[z]
    swung = pltpu.roll(total, 64, 1)
    for a in range(moms):
        at = 3 * (a // 2)
        low, high = (total, swung) if a % 2 == 0 else (swung, total)
        plane[a, 0:1] = jnp.where(lane8[:1] < 64, low[at : at + 1], high[at + 1 : at + 2])
        plane[a, 1:2] = low[at + 2 : at + 3]
    got_p[iy, pair] = plane[me]
    for i, (ry, rx, rm) in enumerate(flats):
        send(remote(
            plane.at[mom_of[rm]], got_p.at[iy, pair], s_p.at[i], r_p.at[iy, pair],
            mom_of[rm], (y_of[ry] * nz + iz) * NX + ix_of[rx],
        ))

    for a in range(moms):
        landed(gl_r.at[0, a], r_gl.at[0, a])
    spread_rows(0, has_low)
    window(0, 0)
    window_tail(0)
    for i in range(NX):
        tail = sum(moved(acc_tail[m], TAIL * i, TAIL * m) for m in range(3))
        hi, lo = zip(*[split(x) for x in (acc[i, 0], acc[i, 1], acc[i, 2], tail)])
        hi, lo = jnp.concatenate(hi, axis=1), jnp.concatenate(lo, axis=1)
        se = jnp.dot(hi, ks_hi[...], preferred_element_type=F32)
        se = se + jnp.dot(lo, ks_hi[...], preferred_element_type=F32)
        se = se + jnp.dot(hi, ks_lo[...], preferred_element_type=F32)
        tail = jnp.dot(hi, ks_tail[...], preferred_element_type=F32)
        tail = tail + jnp.dot(lo, ks_tail[...], preferred_element_type=F32)
        tail = tail + pltpu.roll(tail, 128 - TAIL, 1)
        se = jnp.concatenate([se, tail], axis=1)
        for a in range(moms):
            x = se[rows * a : rows * (a + 1)]
            se_t[i, a, :rows, :] = x[:, :MAIN].astype(BF)
            se_t[i, a, rows:, :] = pack_tail(x[:, MAIN:]).astype(BF)
    for i, (rx, rm) in enumerate(mates):
        if i:
            send(remote(
                se_t.at[ix_of[rx], mom_of[rm]], se_r.at[pair], s_se.at[i], r_se.at[pair],
                mom_of[rm], ring * NX + ix_of[rx],
            ))
    se_r[pair] = se_t[ix, me]

    for i, (rx, rm) in enumerate(mates):
        if i:
            at = mom_of[rm] * NX + ix_of[rx]
            landed(se_r.at[at], r_se.at[at])
    for p in range(pairs):
        at = pl.ds(p, rows, stride=pairs)
        rows_f.at[0][at, :] = se_r[p, :rows, :128].astype(F32)
        rows_f.at[1][at, :] = se_r[p, :rows, 128:].astype(F32)
        tails = unpack_tail(se_r[p, rows:, :].astype(F32))
        rows_f.at[2][at, :] = jnp.concatenate(tails, axis=0)
    whole = jnp.concatenate([rows_f[0], rows_f[1], rows_f[2, :, :TAIL]], axis=1)
    se_ref[...] = whole.reshape(own_k, own_e, pairs, 2 * NN).astype(BF)

    for ry, rx, rm in flats:
        at = (y_of[ry], mom_of[rm] * NX + ix_of[rx])
        landed(got_p.at[at[0], at[1]], r_p.at[at[0], at[1]])
    own_q = momenta // moms
    for p in range(pairs):
        total = got_p[0, p]
        for y in range(1, ny):
            total = total + got_p[y, p]
        for q in range(own_q):
            for m in range(3):
                at = 64 * (m % 2) + 32 * q
                y = pltpu.roll(total, 128 - at, 1) if at else total
                pol_ref[q, m, p, :] = y[m // 2, :window_n]
    for copy in sent:
        copy.wait_send()


def deliver(se_ref, pol_ref, se_out, pol_out, sems):
    copies = [
        pltpu.make_async_copy(se_ref, se_out, sems.at[0]),
        pltpu.make_async_copy(pol_ref, pol_out, sems.at[1]),
    ]
    for copy in copies:
        copy.start()
    for copy in copies:
        copy.wait()


def body(green_less, green_greater, derivative, neighbours, phonon):
    own_k, own_e, pairs, width = green_less.shape
    momenta, window_n = phonon.shape[1], phonon.shape[2]
    moms, ens = lax.axis_size("mom"), lax.axis_size("en")
    nz = min(8, ens // NX)
    ny = ens // (nz * NX)
    dims = (moms, ens, ny, nz, own_k, own_e, pairs, momenta, window_n)
    mates = moms * NX
    span = 32 * momenta
    rows = own_k * own_e
    all_rows = momenta * own_e
    sent = rows + 8
    constants = [jnp.asarray(t, BF) for t in tables()]
    dma = pltpu.SemaphoreType.DMA
    operands = [
        green_less, green_greater, derivative.transpose(1, 0, 2), neighbours,
        phonon.transpose(0, 1, 3, 4, 2), *constants,
    ]
    order = [0, 1, 2, 4, 5, 6]
    near = [pltpu.VMEM(operands[i].shape, operands[i].dtype) for i in order]
    near.insert(3, pltpu.SMEM(neighbours.shape, neighbours.dtype))
    self_energy, pol = pl.pallas_call(
        functools.partial(kernel, dims),
        out_shape=(
            pltpu.VMEM((own_k, own_e, pairs, width), BF),
            pltpu.VMEM((momenta // moms, 3, pairs, window_n), F32),
        ),
        in_specs=[pl.BlockSpec(memory_space=pl.ANY)] * len(operands),
        out_specs=(pl.BlockSpec(memory_space=pltpu.VMEM),) * 2,
        scratch_shapes=near + [
            pltpu.VMEM((3, rows * pairs, 128), F32),
            pltpu.VMEM((pairs, sent, MAIN), BF),
            pltpu.VMEM((pairs, sent, MAIN), BF),
            pltpu.VMEM((4, moms, sent, MAIN), BF),
            pltpu.VMEM((NX, moms, sent, MAIN), BF),
            pltpu.VMEM((4, momenta, 32, MAIN), BF),
            pltpu.VMEM((3, momenta, 32, 128), BF),
            pltpu.VMEM((NX, all_rows, 128), BF),
            pltpu.VMEM((4, 2, 3 * pairs, 128), F32),
            pltpu.VMEM((3, 3 * all_rows, span), BF),
            pltpu.VMEM((3 * MAIN + 128, MAIN), BF),
            pltpu.VMEM((3 * MAIN + 128, MAIN), BF),
            pltpu.VMEM((3 * MAIN + 128, 128), BF),
            pltpu.VMEM((2 * MAIN + 128, 3 * MAIN + 128), BF),
            pltpu.VMEM((NX, 3, all_rows, MAIN), BF),
            pltpu.VMEM((NX, 3, all_rows, 128), BF),
            pltpu.VMEM((NX, 3, all_rows, MAIN), F32),
            pltpu.VMEM((3, all_rows, 128), F32),
            pltpu.VMEM((NX, moms, sent, MAIN), BF),
            pltpu.VMEM((pairs, sent, MAIN), BF),
            pltpu.VMEM((8, 128), F32),
            pltpu.VMEM((nz, 8, 128), F32),
            pltpu.VMEM((moms, 2, 128), F32),
            pltpu.VMEM((ny, pairs, 2, 128), F32),
            dma((len(operands),)), dma((mates,)), dma((NX, moms)), dma((mates,)), dma((mates,)),
            dma((4, moms)), dma((mates,)), dma((pairs,)), dma((nz,)), dma((nz,)),
            dma((ny * mates,)), dma((ny, pairs)),
            pltpu.SemaphoreType.REGULAR, pltpu.SemaphoreType.REGULAR,
        ],
        compiler_params=pltpu.CompilerParams(collective_id=0, has_side_effects=True),
    )(*operands)
    self_energy = pltpu.with_memory_space_constraint(self_energy, pltpu.VMEM)
    pol = pltpu.with_memory_space_constraint(pol, pltpu.VMEM)
    self_energy, pol = pl.pallas_call(
        deliver,
        out_shape=tuple(jax.ShapeDtypeStruct(x.shape, x.dtype) for x in (self_energy, pol)),
        in_specs=[pl.BlockSpec(memory_space=pltpu.VMEM)] * 2,
        out_specs=(pl.BlockSpec(memory_space=pl.ANY),) * 2,
        scratch_shapes=[dma((2,))],
        compiler_params=pltpu.CompilerParams(vmem_limit_bytes=16 << 20),
    )(self_energy, pol)
    return self_energy, pol.transpose(0, 3, 1, 2)


def solution(mesh):
    return jax.shard_map(
        body,
        mesh=mesh,
        in_specs=(P("mom", "en", None, None), P("mom", "en", None, None), P(), P(), P()),
        out_specs=(P("mom", "en", None, None), P("mom", None, None, None)),
        check_vma=False,
    )
```
